128 devices in a mesh: wide: 32 (over y_lo, x, z), narrow: 4 (over y_hi, core).
Axes of the slice: x: 4, y: 4 (y_hi: 2, y_lo: 2; y = y_hi * 2 + y_lo), z: 4, core: 2. Of those that a mesh axis runs over, the one named last changes fastest.
Arguments:
- trial_x: float32 [262144, 128], P(('wide', 'narrow')), may hold values from -6 to 6
- trial_y: float32 [262144, 128], P(('wide', 'narrow')), may hold values from -6 to 6
- energy: float32 [262144], P(('wide', 'narrow')), may hold values from 1 to 4
- level_shift: float32 [128], replicated, may hold values from 0.1 to 0.5
- resonant_kernel: bfloat16 [1024, 8, 256, 256], P(('wide', 'narrow')), may hold values from -0.0625 to 0.0625
- resonant_list: int32 [1024, 8], P(('wide', 'narrow')), may hold values from 0 to 31, all different within a row
- coupling_kernel: bfloat16 [1024, 8, 256, 256], P(('wide', 'narrow')), may hold values from -0.0625 to 0.0625
- coupling_list: int32 [1024, 8], P(('wide', 'narrow')), may hold values from 0 to 31, all different within a row
- partner: int32 [32, 8192], P('wide'), may hold values from 0 to 8191, each once within a row
- exchange_basis: bfloat16 [262144, 1024], P(('wide', 'narrow')), may hold values from -0.0234375 to 0.0234375
Outputs:
- new_x: float32 [262144, 128], P(('wide', 'narrow'))
- new_y: float32 [262144, 128], P(('wide', 'narrow'))
The draws below stay inside these ranges and needn't reach their ends.
Inputs may be any that keep to these rules, and one draw needn't show every extreme that they name: `resonant_list`: each row lists 8 different column blocks. `coupling_list`: each row lists 8 different column blocks. `partner`: each row is a permutation of the patch rows.
All inputs are finite; a program needn't handle non-finite values.
Results may differ from the reference program's by a relative error of at most 0.0038.
Values may be sent and summed in bfloat16 or wider, within the bound.
No kernel may reach another device: no remote copies, remote signals or barrier semaphores. Data moves between devices by JAX's collectives and lax.ppermute only.
A program may use at most 128 MiB of HBM per device.

```python
import jax
import jax.numpy as jnp
from jax import lax

NV = 128
BLK = 256
NBLK = 8
R = 1024
APPS = 2
PATCH = 8192
PAIRS = 262144
N_WIDE = 32


def shard_levels(rng, shape, cuts, smallest, top_value):
    def one(position, shards_of):
        draws = jax.random.uniform(jax.random.fold_in(jax.random.fold_in(rng, 6), position), (shards_of,), jnp.float32, smallest / len(cuts), top_value / len(cuts))
        return jnp.repeat(jnp.exp(draws), shape[position] // shards_of).reshape((-1,) + (1,) * (len(shape) - position - 1))

    level = one(*cuts[0])
    for cut in cuts[1:]:
        level = level * one(*cut)
    return level


def choose_distinct(own_key, rows, number_of, top, lift):
    ranking = jax.random.permutation(jax.random.fold_in(own_key, 1), number_of)
    boost = ranking
    for power in range(3):
        boost = boost * boost // number_of
    boost = boost * lift // number_of
    tickets = jax.random.randint(jax.random.fold_in(own_key, 2), (rows, number_of), 0, 4096) + boost
    sure = jax.random.permutation(jax.random.fold_in(own_key, 3), rows)[jnp.arange(number_of) % rows]
    tickets = jnp.where(jnp.arange(rows)[:, None] == sure[None, :], 1 << 14, tickets)
    merit = tickets * number_of + jnp.arange(number_of)
    return lax.top_k(merit.astype(jnp.int32), top)[1].astype(jnp.int32)


def scatter_about(own_key, shape, deviation, limit, pieces=(), held_as=jnp.bfloat16):
    array = deviation * jax.random.normal(own_key, shape, jnp.float32)
    if pieces:
        array = array * shard_levels(own_key, shape, pieces, -0.22, 0.18)
    return jnp.clip(array, -limit, limit).astype(held_as)


def setup_inputs(seed: int = 0) -> dict:
    arg_keys = jax.random.split(jax.random.key(seed), 11)
    return {
        "trial_x": scatter_about(arg_keys[0], (PAIRS, NV), 1.0, 6.0, ((0, 128),), jnp.float32),
        "trial_y": scatter_about(arg_keys[1], (PAIRS, NV), 1.0, 6.0, ((0, 128),), jnp.float32),
        "energy": jnp.clip(1.0 + 3.0 * jax.random.uniform(arg_keys[2], (PAIRS,), jnp.float32) ** shard_levels(arg_keys[2], (PAIRS,), ((0, 128),), -0.2, 0.2), 1.0, 4.0),
        "level_shift": jnp.clip(jax.random.uniform(arg_keys[3], (NV,), jnp.float32, 0.1, 0.5), 0.1, 0.5),
        "resonant_kernel": scatter_about(arg_keys[4], (PAIRS // BLK, NBLK, BLK, BLK), (NBLK * BLK * 4) ** -0.5, 0.0625, ((0, 128),)),
        "resonant_list": choose_distinct(arg_keys[5], (PAIRS // BLK), PATCH // BLK, NBLK, 0),
        "coupling_kernel": scatter_about(arg_keys[6], (PAIRS // BLK, NBLK, BLK, BLK), (NBLK * BLK * 4) ** -0.5, 0.0625, ((0, 128),)),
        "coupling_list": choose_distinct(arg_keys[7], (PAIRS // BLK), PATCH // BLK, NBLK, 0),
        "partner": jax.vmap(lambda own: jax.random.permutation(own, PATCH))(jax.random.split(arg_keys[8], N_WIDE)).reshape((N_WIDE, PATCH)).astype(jnp.int32),
        "exchange_basis": scatter_about(arg_keys[9], (PAIRS, R), (PAIRS // 4) ** -0.5, 0.0234375, ((0, 128),)),
    }


def patch_products(operands):
    own_patch, mirror_patch, res_kernel, res_list, cp_kernel, cp_list, perm_row = operands
    columns = own_patch.shape[1]
    offsets = jnp.arange(BLK, dtype=jnp.int32)
    own_tiles = own_patch[(res_list[:, :, None] * BLK + offsets).astype(jnp.int32)].astype(jnp.float32)
    mirror_tiles = mirror_patch[perm_row.reshape(-1, BLK)[cp_list]].astype(jnp.float32)
    resonant = jnp.einsum("bnij,bnjc->bic", res_kernel.astype(jnp.float32), own_tiles)
    coupling = jnp.einsum("bnij,bnjc->bic", cp_kernel.astype(jnp.float32), mirror_tiles)
    return resonant.reshape(-1, columns), coupling.reshape(-1, columns)


def apply_once(trial_x, trial_y, energy, level_shift, resonant_kernel, resonant_list, coupling_kernel, coupling_list, partner, exchange_basis):
    vectors = trial_x.shape[1]
    columns = 2 * vectors
    stacked = jnp.concatenate([trial_x.astype(jnp.bfloat16), trial_y.astype(jnp.bfloat16)], axis=1)
    patches = stacked.reshape(N_WIDE, PATCH, columns)
    mirrored = jnp.roll(patches, N_WIDE // 2, axis=0)
    blocks = PATCH // BLK
    res_kernel = resonant_kernel.reshape(N_WIDE, blocks, NBLK, BLK, BLK)
    res_list = resonant_list.reshape(N_WIDE, blocks, NBLK)
    cp_kernel = coupling_kernel.reshape(N_WIDE, blocks, NBLK, BLK, BLK)
    cp_list = coupling_list.reshape(N_WIDE, blocks, NBLK)
    resonant, coupling = lax.map(patch_products, (patches, mirrored, res_kernel, res_list, cp_kernel, cp_list, partner))
    resonant = resonant.reshape(-1, columns)
    coupling = coupling.reshape(-1, columns)
    summed = (trial_x + trial_y).astype(jnp.bfloat16)
    weights = lax.dot_general(exchange_basis, summed, (((0,), (0,)), ((), ())), preferred_element_type=jnp.float32)
    exchange = jnp.dot(exchange_basis, weights.astype(jnp.bfloat16), preferred_element_type=jnp.float32)
    levels = energy[:, None]
    shifts = level_shift[None, :]
    image_x = levels * trial_x + resonant[:, :vectors] + coupling[:, vectors:] + exchange
    image_y = -(levels * trial_y + resonant[:, vectors:] + coupling[:, :vectors] + exchange)
    next_x = (image_x - shifts * trial_x) / (levels - shifts)
    next_y = -(image_y - shifts * trial_y) / (levels + shifts)
    return next_x, next_y


def reference(trial_x, trial_y, energy, level_shift, resonant_kernel, resonant_list, coupling_kernel, coupling_list, partner, exchange_basis):
    current_x, current_y = trial_x, trial_y
    for app_index in range(APPS):
        current_x, current_y = apply_once(current_x, current_y, energy, level_shift, resonant_kernel, resonant_list, coupling_kernel, coupling_list, partner, exchange_basis)
    return current_x, current_y
```

```python
import jax
import jax.numpy as jnp
from jax import lax
from jax.experimental import pallas as pl
from jax.experimental.pallas import tpu as pltpu
from jax.sharding import PartitionSpec as P

BLK = 256
NV = 128
NBLK = 8
APPS = 2
AXES = ("wide", "narrow")
BF16 = jnp.bfloat16
F32 = jnp.float32
MIB = 1 << 20

VMEM_SPEC = pl.BlockSpec(memory_space=pltpu.VMEM)
SMEM_SPEC = pl.BlockSpec(memory_space=pltpu.SMEM)
ANY_SPEC = pl.BlockSpec(memory_space=pl.ANY)


def toggled(array, mask):
    return lax.ppermute(array, AXES, [(i, i ^ mask) for i in range(lax.axis_size(AXES))])


def interleave(x, y, scratch):
    scratch[pl.ds(0, BLK, stride=2), :] = x
    scratch[pl.ds(1, BLK, stride=2), :] = y
    return scratch[...].astype(BF16)


def split_matrix():
    row = lax.broadcasted_iota(jnp.int32, (BLK, BLK), 0)
    col = lax.broadcasted_iota(jnp.int32, (BLK, BLK), 1)
    half = BLK // 2
    hit = (col == 2 * row) | (col == 2 * (row - half) + 1)
    return jnp.where(hit, 1.0, 0.0).astype(F32).astype(BF16)


def split_block(flat, block, out, select):
    base = pl.multiple_of(block * 2 * BLK, 2 * BLK)
    half = BLK // 2
    pair = jnp.concatenate([flat[pl.ds(base, BLK), :], flat[pl.ds(base + BLK, BLK), :]], axis=1)
    parts = jnp.dot(select, pair, preferred_element_type=F32).astype(BF16)
    out[block, 0:half, 0:NV] = parts[0:half, 0:NV]
    out[block, half:BLK, 0:NV] = parts[0:half, NV:]
    out[block, 0:half, NV:] = parts[half:, 0:NV]
    out[block, half:BLK, NV:] = parts[half:, NV:]


def pack_body(x_ref, y_ref, out_ref, scratch):
    out_ref[...] = interleave(x_ref[...], y_ref[...], scratch)


def pack(x, y):
    rows = x.shape[0]
    block = pl.BlockSpec((BLK, NV), lambda b: (b, 0))
    return pl.pallas_call(
        pack_body,
        grid=(rows // BLK,),
        in_specs=[block, block],
        out_specs=pl.BlockSpec((2 * BLK, NV), lambda b: (b, 0)),
        out_shape=jax.ShapeDtypeStruct((2 * rows, NV), BF16),
        scratch_shapes=[pltpu.VMEM((2 * BLK, NV), F32)],
        name="pack",
    )(x, y)


def project_body(x_ref, y_ref, basis_ref, out_ref):
    @pl.when(pl.program_id(0) == 0)
    def _():
        out_ref[...] = jnp.zeros_like(out_ref)

    summed = (x_ref[...] + y_ref[...]).astype(BF16)
    out_ref[...] += lax.dot_general(
        basis_ref[...], summed, (((0,), (0,)), ((), ())), preferred_element_type=F32
    )


def project(x, y, basis):
    rows, rank = basis.shape
    block = pl.BlockSpec((BLK, NV), lambda b: (b, 0))
    return pl.pallas_call(
        project_body,
        grid=(rows // BLK,),
        in_specs=[block, block, pl.BlockSpec((BLK, rank), lambda b: (b, 0))],
        out_specs=pl.BlockSpec((rank, NV), lambda b: (0, 0)),
        out_shape=jax.ShapeDtypeStruct((rank, NV), F32),
        name="project",
    )(x, y, basis)


def mirror_body(slot_ref, partner_ref, list_ref, *refs):
    chunks = refs[:8]
    kernel_hbm, out_ref, source, gathered, columns, kernel, chunk_sems, kernel_sems = refs[8:]
    rows = chunks[0].shape[0]
    flat = source.reshape(2 * source.shape[0], NV)
    copies = []
    for k in range(8):
        slot = slot_ref[0] ^ (k // 2)
        start = pl.multiple_of(slot * 2 * rows + (k % 2) * rows, rows)
        copies.append(pltpu.make_async_copy(chunks[k], flat.at[pl.ds(start, rows)], chunk_sems.at[k]))
        copies[-1].start()
    blocks = kernel.shape[0]
    loads = [pltpu.make_async_copy(kernel_hbm.at[b], kernel.at[b], kernel_sems.at[b]) for b in range(blocks)]
    for load in loads:
        load.start()
    for copy in copies:
        copy.wait()
    unroll = 64

    def gather(step, carry):
        base = step * unroll
        for u in range(unroll):
            gathered[base + u] = source[partner_ref[0, base + u]]
        return carry

    lax.fori_loop(0, source.shape[0] // unroll, gather, 0)
    select = split_matrix()
    flat_out = gathered.reshape(2 * gathered.shape[0], NV)

    def split(block, carry):
        split_block(flat_out, block, columns, select)
        return carry

    lax.fori_loop(0, columns.shape[0], split, 0, unroll=2)
    for load in loads:
        load.wait()

    def product(b, carry):
        total = jnp.dot(kernel[b, 0], columns[list_ref[b, 0]], preferred_element_type=F32)
        for n in range(1, NBLK):
            total += jnp.dot(kernel[b, n], columns[list_ref[b, n]], preferred_element_type=F32)
        out_ref[b] = total
        return carry

    lax.fori_loop(0, blocks, product, 0)


def mirror_product(slot, partner, indices, chunks, kernel):
    patch = partner.shape[1]
    blocks = kernel.shape[0]
    return pl.pallas_call(
        mirror_body,
        in_specs=[SMEM_SPEC] * 3 + [ANY_SPEC] * 9,
        out_specs=VMEM_SPEC,
        out_shape=jax.ShapeDtypeStruct((blocks, BLK, 2 * NV), F32),
        scratch_shapes=[
            pltpu.VMEM((patch, 2, NV), BF16),
            pltpu.VMEM((patch, 2, NV), BF16),
            pltpu.VMEM((patch // BLK, BLK, 2 * NV), BF16),
            pltpu.VMEM(kernel.shape, BF16),
            pltpu.SemaphoreType.DMA((8,)),
            pltpu.SemaphoreType.DMA((blocks,)),
        ],
        compiler_params=pltpu.CompilerParams(vmem_limit_bytes=40 * MIB),
        name="mirror_product",
    )(slot, partner, indices, *chunks, kernel)


def column_of(row):
    return jnp.broadcast_to(row, (NV, NV)).T


def finish_body(last, slot_ref, list_ref, *refs):
    chunks = refs[:8]
    rest = refs[8:]
    x_ref, y_ref, energy_ref, shift_ref, kernel_ref, basis_ref, weight_ref, mirror_ref = rest[:8]
    if last:
        next_x_ref, next_y_ref, flat, columns, chunk_sems = rest[8:]
    else:
        next_x_ref, next_y_ref, packed_ref, project_ref, flat, columns, chunk_sems, scratch = rest[8:]
    b = pl.program_id(0)
    rows = chunks[0].shape[0]

    @pl.when(b == 0)
    def _():
        copies = []
        for k in range(8):
            slot = slot_ref[0] ^ (k // 2)
            start = pl.multiple_of(slot * 2 * rows + (k % 2) * rows, rows)
            copies.append(pltpu.make_async_copy(chunks[k], flat.at[pl.ds(start, rows)], chunk_sems.at[k]))
            copies[-1].start()
        for copy in copies:
            copy.wait()
        select = split_matrix()

        def split(block, carry):
            split_block(flat, block, columns, select)
            return carry

        lax.fori_loop(0, columns.shape[0], split, 0, unroll=2)
        if not last:
            project_ref[...] = jnp.zeros_like(project_ref)

    total = mirror_ref[0]
    exchange = jnp.dot(basis_ref[...], weight_ref[...], preferred_element_type=F32)
    direct = jnp.dot(kernel_ref[0, 0], columns[list_ref[b, 0]], preferred_element_type=F32)
    for n in range(1, NBLK):
        direct += jnp.dot(kernel_ref[0, n], columns[list_ref[b, n]], preferred_element_type=F32)
    shifts = shift_ref[...]
    half = BLK // 2
    levels = jnp.concatenate([column_of(energy_ref[0, 0:1, 0:half]), column_of(energy_ref[0, 0:1, half:])], axis=0)
    next_x = x_ref[...] + (direct[:, :NV] + total[:, NV:] + exchange) / (levels - shifts)
    next_y = y_ref[...] + (direct[:, NV:] + total[:, :NV] + exchange) / (levels + shifts)
    next_x_ref[...] = next_x
    next_y_ref[...] = next_y
    if not last:
        packed_ref[...] = interleave(next_x, next_y, scratch)
        project_ref[...] += lax.dot_general(
            basis_ref[...], (next_x + next_y).astype(BF16), (((0,), (0,)), ((), ())), preferred_element_type=F32
        )


def finish(last, slot, indices, chunks, x, y, energy, shift, kernel, basis, weights, mirrored):
    rows, rank = basis.shape
    blocks = kernel.shape[0]
    patch = 4 * rows
    vector = pl.BlockSpec((BLK, NV), lambda b: (b, 0))
    out_specs = [vector, vector]
    out_shape = [jax.ShapeDtypeStruct((rows, NV), F32)] * 2
    scratch = [
        pltpu.VMEM((2 * patch, NV), BF16),
        pltpu.VMEM((patch // BLK, BLK, 2 * NV), BF16),
        pltpu.SemaphoreType.DMA((8,)),
    ]
    if not last:
        out_specs += [pl.BlockSpec((2 * BLK, NV), lambda b: (b, 0)), pl.BlockSpec((rank, NV), lambda b: (0, 0))]
        out_shape += [jax.ShapeDtypeStruct((2 * rows, NV), BF16), jax.ShapeDtypeStruct((rank, NV), F32)]
        scratch += [pltpu.VMEM((2 * BLK, NV), F32)]

    def body(*refs):
        finish_body(last, *refs)

    return pl.pallas_call(
        body,
        grid=(blocks,),
        in_specs=[SMEM_SPEC] * 2
        + [ANY_SPEC] * 8
        + [
            vector,
            vector,
            pl.BlockSpec((1, 1, BLK), lambda b: (b, 0, 0)),
            pl.BlockSpec((1, NV), lambda b: (0, 0)),
            pl.BlockSpec((1, NBLK, BLK, BLK), lambda b: (b, 0, 0, 0)),
            pl.BlockSpec((BLK, rank), lambda b: (b, 0)),
            pl.BlockSpec((rank, NV), lambda b: (0, 0)),
            pl.BlockSpec((1, BLK, 2 * NV), lambda b: (b, 0, 0)),
        ],
        out_specs=out_specs,
        out_shape=out_shape,
        scratch_shapes=scratch,
        compiler_params=pltpu.CompilerParams(vmem_limit_bytes=40 * MIB),
        name="finish_last" if last else "finish",
    )(slot, indices, *chunks, x, y, energy, shift, kernel, basis, weights, mirrored)


def total_weights(partial):
    size = lax.axis_size(AXES)
    rank, vectors = partial.shape
    part = rank // size
    pieces = lax.all_to_all(partial.reshape(size, part, vectors), AXES, 0, 0, tiled=True)
    own = jnp.sum(pieces, axis=0).astype(BF16)
    spread = lax.all_to_all(jnp.broadcast_to(own[None], (size, part, vectors)), AXES, 0, 0, tiled=True)
    return spread.reshape(rank, vectors)


def on_device(x, y, energy, shift, res_kernel, res_list, cp_kernel, cp_list, partner, basis):
    size = lax.axis_size(AXES)
    narrow = lax.axis_size("narrow")
    near = size // 2
    far = near | (narrow // 2)
    slot = lax.axis_index("narrow").astype(jnp.int32).reshape(1)
    blocks = res_kernel.shape[0]
    levels = energy.reshape(blocks, 1, BLK)
    shifts = shift.reshape(1, NV)
    packed = pack(x, y)
    partial = project(x, y, basis)
    for app in range(APPS):
        last = app == APPS - 1
        half = packed.shape[0] // 2
        low, high = packed[:half], packed[half:]
        far_low = toggled(low, far)
        near_high = toggled(high, near)
        far_high = toggled(high, far)
        near_low = toggled(low, near)
        own_low, own_high = toggled(low, 1), toggled(high, 1)
        across_low = toggled(far_low, near)
        across_high = toggled(near_high, far)
        first = [near_low, near_high]
        second = [far_low, far_high]
        mirror_chunks = first + [toggled(c, 1) for c in first] + second + [toggled(c, 1) for c in second]
        across = [across_low, across_high]
        own_chunks = [low, high, own_low, own_high] + across + [toggled(c, 1) for c in across]
        weights = total_weights(partial)
        mirrored = mirror_product(slot, partner, cp_list, mirror_chunks, cp_kernel)
        out = finish(
            last, slot, res_list, own_chunks, x, y, levels, shifts, res_kernel, basis, weights, mirrored
        )
        if last:
            return tuple(out)
        x, y, packed, partial = out


def solution(mesh):
    return jax.shard_map(
        on_device,
        mesh=mesh,
        in_specs=(
            P(AXES, None),
            P(AXES, None),
            P(AXES),
            P(),
            P(AXES, None, None, None),
            P(AXES, None),
            P(AXES, None, None, None),
            P(AXES, None),
            P("wide", None),
            P(AXES, None),
        ),
        out_specs=(P(AXES, None), P(AXES, None)),
        check_vma=False,
    )
```

```python
import jax
import jax.numpy as jnp
from jax import lax
from jax.experimental import pallas as pl
from jax.experimental.pallas import tpu as pltpu
from jax.sharding import PartitionSpec as P


BLK = 256
NV = 128
NBLK = 8
APPS = 2
AXES = ("wide", "narrow")
BF16 = jnp.bfloat16
F32 = jnp.float32
MIB = 1 << 20


VMEM_SPEC = pl.BlockSpec(memory_space=pltpu.VMEM)
SMEM_SPEC = pl.BlockSpec(memory_space=pltpu.SMEM)
ANY_SPEC = pl.BlockSpec(memory_space=pl.ANY)


def toggled(array, mask):
    return lax.ppermute(array, AXES, [(i, i ^ mask) for i in range(lax.axis_size(AXES))])


def interleave(x, y, scratch):
    scratch[pl.ds(0, x.shape[0], stride=2), :] = x
    scratch[pl.ds(1, x.shape[0], stride=2), :] = y
    return scratch[...].astype(BF16)


def in_hbm(*arrays):
    return [pltpu.with_memory_space_constraint(a, pltpu.HBM) for a in arrays]


def block_rows(b, size=BLK):
    return pl.ds(pl.multiple_of(b * size, size), size)


def split_matrix():
    row = lax.broadcasted_iota(jnp.int32, (BLK, BLK), 0)
    col = lax.broadcasted_iota(jnp.int32, (BLK, BLK), 1)
    half = BLK // 2
    hit = (col == 2 * row) | (col == 2 * (row - half) + 1)
    return jnp.where(hit, 1.0, 0.0).astype(F32).astype(BF16)


def split_block(flat, block, out, select):
    base = pl.multiple_of(block * 2 * BLK, 2 * BLK)
    half = BLK // 2
    pair = jnp.concatenate([flat[pl.ds(base, BLK), :], flat[pl.ds(base + BLK, BLK), :]], axis=1)
    parts = jnp.dot(select, pair, preferred_element_type=F32).astype(BF16)
    out[block, 0:half, 0:NV] = parts[0:half, 0:NV]
    out[block, half:BLK, 0:NV] = parts[0:half, NV:]
    out[block, 0:half, NV:] = parts[half:, 0:NV]
    out[block, half:BLK, NV:] = parts[half:, NV:]


def pack_body(x_hbm, y_hbm, low_ref, high_ref, x, y, scratch, sems):
    size = scratch.shape[0] // 2
    parts = x.shape[0] // size
    loads = []
    for p in range(parts):
        for t, (source, target) in enumerate(((x_hbm, x), (y_hbm, y))):
            rows = pl.ds(p * size, size)
            loads.append(pltpu.make_async_copy(source.at[rows], target.at[rows], sems.at[2 * p + t]))
            loads[-1].start()
    for p in range(parts):
        loads[2 * p].wait()
        loads[2 * p + 1].wait()
        rows = pl.ds(p * size, size)
        out, place = (low_ref, p) if p < parts // 2 else (high_ref, p - parts // 2)
        out[pl.ds(place * 2 * size, 2 * size), :] = interleave(x[rows, :], y[rows, :], scratch)


def pack(x, y):
    rows = x.shape[0]
    parts = 4
    return pl.pallas_call(
        pack_body,
        in_specs=[ANY_SPEC, ANY_SPEC],
        out_specs=[VMEM_SPEC, VMEM_SPEC],
        out_shape=[jax.ShapeDtypeStruct((rows, NV), BF16)] * 2,
        scratch_shapes=[
            pltpu.VMEM((rows, NV), F32),
            pltpu.VMEM((rows, NV), F32),
            pltpu.VMEM((2 * rows // parts, NV), F32),
            pltpu.SemaphoreType.DMA((2 * parts,)),
        ],
        compiler_params=pltpu.CompilerParams(vmem_limit_bytes=8 * MIB),
        name="pack",
    )(*in_hbm(x, y))


def add_projection(total, first, x, y, basis):
    value = jnp.dot((x + y).T.astype(BF16), basis, preferred_element_type=F32)

    @pl.when(first)
    def _():
        total[...] = value

    @pl.when(jnp.logical_not(first))
    def _():
        total[...] += value


def store_projection(total, out_ref):
    for r in range(total.shape[1] // NV):
        out_ref[r * NV : (r + 1) * NV, :] = total[:, r * NV : (r + 1) * NV].T.astype(BF16)


def project_body(x_hbm, y_hbm, basis_hbm, out_ref, x, y, basis, total, sems):
    size = BLK
    blocks = x.shape[0] // size
    triples = ((x_hbm, x), (y_hbm, y), (basis_hbm, basis))

    def load(b, t):
        source, target = triples[t]
        rows = block_rows(b)
        return pltpu.make_async_copy(source.at[rows], target.at[rows], sems.at[t, b])

    for b in range(blocks):
        for t in range(3):
            load(b, t).start()

    def step(b, carry):
        for t in range(3):
            load(b, t).wait()
        rows = block_rows(b)
        add_projection(total, b == 0, x[rows, :], y[rows, :], basis[rows, :])
        return carry

    lax.fori_loop(0, blocks, step, 0)
    store_projection(total, out_ref)


def project(x, y, basis):
    rows, rank = basis.shape
    return pl.pallas_call(
        project_body,
        in_specs=[ANY_SPEC] * 3,
        out_specs=VMEM_SPEC,
        out_shape=pltpu.HBM((rank, NV), BF16),
        scratch_shapes=[
            pltpu.VMEM((rows, NV), F32),
            pltpu.VMEM((rows, NV), F32),
            pltpu.VMEM((rows, rank), BF16),
            pltpu.VMEM((NV, rank), F32),
            pltpu.SemaphoreType.DMA((3, rows // BLK)),
        ],
        compiler_params=pltpu.CompilerParams(vmem_limit_bytes=12 * MIB),
        name="project",
    )(*in_hbm(x, y, basis))


def list_product(kernel, columns, list_ref, b):
    left = jnp.concatenate([kernel[b, n] for n in range(NBLK)], axis=1)
    right = jnp.concatenate([columns[list_ref[b, n]] for n in range(NBLK)], axis=0)
    return jnp.dot(left, right, preferred_element_type=F32)


def load_patch(slot_ref, chunks, flat, sems):
    rows = chunks[0].shape[0]
    copies = []
    for k, chunk in enumerate(chunks):
        slot = slot_ref[0] ^ (k // 2)
        start = pl.multiple_of(slot * 2 * rows + (k % 2) * rows, rows)
        copies.append(pltpu.make_async_copy(chunk, flat.at[pl.ds(start, rows)], sems.at[k]))
        copies[-1].start()
    return copies


def gather_body(slot_ref, partner_ref, *refs):
    chunks = refs[:8]
    columns_ref, source, gathered, sems = refs[8:]
    for copy in load_patch(slot_ref, chunks, source.reshape(2 * source.shape[0], NV), sems):
        copy.wait()
    unroll = 64

    def gather(step, carry):
        base = step * unroll
        for u in range(unroll):
            gathered[base + u] = source[partner_ref[0, base + u]]
        return carry

    lax.fori_loop(0, source.shape[0] // unroll, gather, 0)
    select = split_matrix()
    flat_out = gathered.reshape(2 * gathered.shape[0], NV)

    def split(block, carry):
        split_block(flat_out, block, columns_ref, select)
        return carry

    lax.fori_loop(0, columns_ref.shape[0], split, 0, unroll=8)


def mirror_columns(slot, partner, chunks):
    patch = partner.shape[1]
    return pl.pallas_call(
        gather_body,
        in_specs=[SMEM_SPEC] * 2 + [ANY_SPEC] * 8,
        out_specs=VMEM_SPEC,
        out_shape=jax.ShapeDtypeStruct((patch // BLK, BLK, 2 * NV), BF16),
        scratch_shapes=[
            pltpu.VMEM((patch, 2, NV), BF16),
            pltpu.VMEM((patch, 2, NV), BF16),
            pltpu.SemaphoreType.DMA((8,)),
        ],
        compiler_params=pltpu.CompilerParams(vmem_limit_bytes=16 * MIB),
        name="mirror_columns",
    )(slot, partner, *in_hbm(*chunks))


def product_body(list_ref, columns_ref, kernel_hbm, out_ref, kernel, sems):
    blocks = kernel.shape[0]

    def load(b):
        return pltpu.make_async_copy(kernel_hbm.at[b], kernel.at[b], sems.at[b])

    for b in range(blocks):
        load(b).start()

    def step(b, carry):
        load(b).wait()
        out_ref[b] = list_product(kernel, columns_ref, list_ref, b)
        return carry

    lax.fori_loop(0, blocks, step, 0)


def mirror_product(indices, columns, kernel):
    blocks = kernel.shape[0]
    return pl.pallas_call(
        product_body,
        in_specs=[SMEM_SPEC, VMEM_SPEC, ANY_SPEC],
        out_specs=VMEM_SPEC,
        out_shape=jax.ShapeDtypeStruct((blocks, BLK, 2 * NV), F32),
        scratch_shapes=[pltpu.VMEM(kernel.shape, BF16), pltpu.SemaphoreType.DMA((blocks,))],
        compiler_params=pltpu.CompilerParams(vmem_limit_bytes=16 * MIB),
        name="mirror_product",
    )(indices, columns, *in_hbm(kernel))


def column_of(row):
    return jnp.broadcast_to(row, (NV, NV)).T


def finish_body(last, slot_ref, list_ref, *refs):
    chunks = refs[:8]
    x_hbm, y_hbm, energy_ref, shift_ref, kernel_hbm, basis_hbm, weight_ref, mirror_ref = refs[8:16]
    rest = refs[16:]
    if last:
        next_x_hbm, next_y_hbm = rest[:2]
        flat, columns, kernel, basis, x, y, chunk_sems, sems = rest[2:]
    else:
        next_x_hbm, next_y_hbm, low_ref, high_ref, project_ref = rest[:5]
        flat, columns, kernel, basis, x, y, chunk_sems, sems, scratch, total = rest[5:]
    blocks = kernel.shape[0]
    copies = load_patch(slot_ref, chunks, flat, chunk_sems)

    def load(b, t):
        if t == 0:
            return pltpu.make_async_copy(kernel_hbm.at[b], kernel.at[b], sems.at[0, b])
        source, target = ((basis_hbm, basis), (x_hbm, x), (y_hbm, y))[t - 1]
        part = block_rows(b)
        return pltpu.make_async_copy(source.at[part], target.at[part], sems.at[t, b])

    def save(b, t):
        source, target = ((x, next_x_hbm), (y, next_y_hbm))[t]
        part = block_rows(b)
        return pltpu.make_async_copy(source.at[part], target.at[part], sems.at[2 + t, b])

    for b in range(blocks):
        for t in range(4):
            load(b, t).start()
    for copy in copies:
        copy.wait()
    select = split_matrix()

    def split(block, carry):
        split_block(flat, block, columns, select)
        return carry

    lax.fori_loop(0, columns.shape[0], split, 0, unroll=8)
    shifts = shift_ref[...]
    half = BLK // 2

    def step(b, carry):
        for t in range(4):
            load(b, t).wait()
        part = block_rows(b)
        mirrored = mirror_ref[b]
        exchange = jnp.dot(basis[part, :], weight_ref[...], preferred_element_type=F32)
        direct = list_product(kernel, columns, list_ref, b)
        row = energy_ref[b]
        levels = jnp.concatenate([column_of(row[:, 0:half]), column_of(row[:, half:])], axis=0)
        next_x = x[part, :] + (direct[:, :NV] + mirrored[:, NV:] + exchange) / (levels - shifts)
        next_y = y[part, :] + (direct[:, NV:] + mirrored[:, :NV] + exchange) / (levels + shifts)
        x[part, :] = next_x
        y[part, :] = next_y
        for t in range(2):
            save(b, t).start()
        if not last:
            mixed = interleave(next_x, next_y, scratch)
            place = pl.ds(pl.multiple_of((b % (blocks // 2)) * 2 * BLK, 2 * BLK), 2 * BLK)

            @pl.when(b < blocks // 2)
            def _():
                low_ref[place, :] = mixed

            @pl.when(b >= blocks // 2)
            def _():
                high_ref[place, :] = mixed

            add_projection(total, b == 0, next_x, next_y, basis[part, :])
        return carry

    lax.fori_loop(0, blocks, step, 0)
    if not last:
        store_projection(total, project_ref)
    for b in range(blocks):
        for t in range(2):
            save(b, t).wait()


def finish(last, slot, indices, chunks, x, y, energy, shift, kernel, basis, weights, mirrored):
    rows, rank = basis.shape
    blocks = kernel.shape[0]
    patch = 4 * rows
    out_specs = [ANY_SPEC, ANY_SPEC]
    out_shape = [pltpu.HBM((rows, NV), F32)] * 2
    scratch = [
        pltpu.VMEM((2 * patch, NV), BF16),
        pltpu.VMEM((patch // BLK, BLK, 2 * NV), BF16),
        pltpu.VMEM(kernel.shape, BF16),
        pltpu.VMEM(basis.shape, BF16),
        pltpu.VMEM((rows, NV), F32),
        pltpu.VMEM((rows, NV), F32),
        pltpu.SemaphoreType.DMA((8,)),
        pltpu.SemaphoreType.DMA((4, blocks)),
    ]
    if not last:
        out_specs += [VMEM_SPEC] * 3
        out_shape += [jax.ShapeDtypeStruct((rows, NV), BF16)] * 2 + [pltpu.HBM((rank, NV), BF16)]
        scratch += [pltpu.VMEM((2 * BLK, NV), F32), pltpu.VMEM((NV, rank), F32)]

    def body(*refs):
        finish_body(last, *refs)

    return pl.pallas_call(
        body,
        in_specs=[SMEM_SPEC] * 2 + [ANY_SPEC] * 10 + [VMEM_SPEC] * 2 + [ANY_SPEC] * 2 + [VMEM_SPEC] * 2,
        out_specs=out_specs,
        out_shape=out_shape,
        scratch_shapes=scratch,
        compiler_params=pltpu.CompilerParams(vmem_limit_bytes=32 * MIB),
        name="finish_last" if last else "finish",
    )(slot, indices, *in_hbm(*chunks, x, y), energy, shift, *in_hbm(kernel, basis), weights, mirrored)


def total_weights(partial):
    size = lax.axis_size(AXES)
    rank, vectors = partial.shape
    part = rank // size
    pieces = lax.all_to_all(partial.reshape(size, part, vectors), AXES, 0, 0, tiled=True)
    own = jnp.sum(pieces.astype(F32), axis=0).astype(BF16)
    spread = lax.all_to_all(jnp.broadcast_to(own[None], (size, part, vectors)), AXES, 0, 0, tiled=True)
    return spread.reshape(rank, vectors)


def on_device(x, y, energy, shift, res_kernel, res_list, cp_kernel, cp_list, partner, basis):
    size = lax.axis_size(AXES)
    narrow = lax.axis_size("narrow")
    near = size // 2
    far = near | (narrow // 2)
    slot = lax.axis_index("narrow").astype(jnp.int32).reshape(1)
    blocks = res_kernel.shape[0]
    levels = energy.reshape(blocks, 1, BLK)
    shifts = shift.reshape(1, NV)
    for app in range(APPS):
        last = app == APPS - 1
        if app == 0:
            low, high = pack(x, y)
            partial = project(x, y, basis)
        far_low = toggled(low, far)
        near_high = toggled(high, near)
        far_high = toggled(high, far)
        near_low = toggled(low, near)
        own = [toggled(low, 1), toggled(high, 1)]
        across = [toggled(far_low, near), toggled(near_high, far)]
        mirror_chunks = [near_low, near_high]
        mirror_chunks += [toggled(c, 1) for c in mirror_chunks]
        mirror_chunks += [far_low, far_high]
        mirror_chunks += [toggled(c, 1) for c in mirror_chunks[4:]]
        own_chunks = [low, high] + own + across + [toggled(c, 1) for c in across]
        weights = total_weights(partial)
        mirror = mirror_columns(slot, partner, mirror_chunks)
        mirrored = mirror_product(cp_list, mirror, cp_kernel)
        out = finish(
            last, slot, res_list, own_chunks, x, y, levels, shifts, res_kernel, basis, weights, mirrored
        )
        if last:
            return tuple(out)
        x, y, low, high, partial = out


def solution(mesh):
    return jax.shard_map(
        on_device,
        mesh=mesh,
        in_specs=(
            P(AXES, None),
            P(AXES, None),
            P(AXES),
            P(),
            P(AXES, None, None, None),
            P(AXES, None),
            P(AXES, None, None, None),
            P(AXES, None),
            P("wide", None),
            P(AXES, None),
        ),
        out_specs=(P(AXES, None), P(AXES, None)),
        check_vma=False,
    )
```

```python
import jax
import jax.numpy as jnp
from jax import lax
from jax.experimental import pallas as pl
from jax.experimental.pallas import tpu as pltpu
from jax.sharding import PartitionSpec as P


BLK = 256
NV = 128
NBLK = 8
APPS = 2
AXES = ("wide", "narrow")
BF16 = jnp.bfloat16
F32 = jnp.float32
MIB = 1 << 20


VMEM_SPEC = pl.BlockSpec(memory_space=pltpu.VMEM)
SMEM_SPEC = pl.BlockSpec(memory_space=pltpu.SMEM)
ANY_SPEC = pl.BlockSpec(memory_space=pl.ANY)


def toggled(array, mask):
    return lax.ppermute(array, AXES, [(i, i ^ mask) for i in range(lax.axis_size(AXES))])


def interleave(x, y, scratch):
    scratch[pl.ds(0, x.shape[0], stride=2), :] = x
    scratch[pl.ds(1, x.shape[0], stride=2), :] = y
    return scratch[...].astype(BF16)


def in_hbm(*arrays):
    return [pltpu.with_memory_space_constraint(a, pltpu.HBM) for a in arrays]


def block_rows(b, size=BLK):
    return pl.ds(pl.multiple_of(b * size, size), size)


def split_matrix():
    row = lax.broadcasted_iota(jnp.int32, (BLK, BLK), 0)
    col = lax.broadcasted_iota(jnp.int32, (BLK, BLK), 1)
    half = BLK // 2
    hit = (col == 2 * row) | (col == 2 * (row - half) + 1)
    return jnp.where(hit, 1.0, 0.0).astype(F32).astype(BF16)


def split_block(flat, block, out, select):
    base = pl.multiple_of(block * 2 * BLK, 2 * BLK)
    half = BLK // 2
    pair = jnp.concatenate([flat[pl.ds(base, BLK), :], flat[pl.ds(base + BLK, BLK), :]], axis=1)
    parts = jnp.dot(select, pair, preferred_element_type=F32).astype(BF16)
    out[block, 0:half, 0:NV] = parts[0:half, 0:NV]
    out[block, half:BLK, 0:NV] = parts[0:half, NV:]
    out[block, 0:half, NV:] = parts[half:, 0:NV]
    out[block, half:BLK, NV:] = parts[half:, NV:]


def pack_body(x_hbm, y_hbm, low_ref, high_ref, x, y, scratch, sems):
    size = scratch.shape[0] // 2
    parts = x.shape[0] // size
    loads = []
    for p in range(parts):
        for t, (source, target) in enumerate(((x_hbm, x), (y_hbm, y))):
            rows = pl.ds(p * size, size)
            loads.append(pltpu.make_async_copy(source.at[rows], target.at[rows], sems.at[2 * p + t]))
            loads[-1].start()
    for p in range(parts):
        loads[2 * p].wait()
        loads[2 * p + 1].wait()
        rows = pl.ds(p * size, size)
        out, place = (low_ref, p) if p < parts // 2 else (high_ref, p - parts // 2)
        out[pl.ds(place * 2 * size, 2 * size), :] = interleave(x[rows, :], y[rows, :], scratch)


def pack(x, y):
    rows = x.shape[0]
    parts = 4
    return pl.pallas_call(
        pack_body,
        in_specs=[ANY_SPEC, ANY_SPEC],
        out_specs=[VMEM_SPEC, VMEM_SPEC],
        out_shape=[jax.ShapeDtypeStruct((rows, NV), BF16)] * 2,
        scratch_shapes=[
            pltpu.VMEM((rows, NV), F32),
            pltpu.VMEM((rows, NV), F32),
            pltpu.VMEM((2 * rows // parts, NV), F32),
            pltpu.SemaphoreType.DMA((2 * parts,)),
        ],
        compiler_params=pltpu.CompilerParams(vmem_limit_bytes=8 * MIB),
        name="pack",
    )(*in_hbm(x, y))


def add_projection(total, first, x, y, basis):
    value = jnp.dot((x + y).T.astype(BF16), basis, preferred_element_type=F32)

    @pl.when(first)
    def _():
        total[...] = value

    @pl.when(jnp.logical_not(first))
    def _():
        total[...] += value


def store_projection(total, out_ref):
    for r in range(total.shape[1] // NV):
        out_ref[r * NV : (r + 1) * NV, :] = total[:, r * NV : (r + 1) * NV].T


def project_body(x_hbm, y_hbm, basis_hbm, out_ref, x, y, basis, total, sems):
    size = BLK
    blocks = x.shape[0] // size
    triples = ((x_hbm, x), (y_hbm, y), (basis_hbm, basis))

    def load(b, t):
        source, target = triples[t]
        rows = block_rows(b)
        return pltpu.make_async_copy(source.at[rows], target.at[rows], sems.at[t, b])

    for b in range(blocks):
        for t in range(3):
            load(b, t).start()

    def step(b, carry):
        for t in range(3):
            load(b, t).wait()
        rows = block_rows(b)
        add_projection(total, b == 0, x[rows, :], y[rows, :], basis[rows, :])
        return carry

    lax.fori_loop(0, blocks, step, 0)
    store_projection(total, out_ref)


def project(x, y, basis):
    rows, rank = basis.shape
    return pl.pallas_call(
        project_body,
        in_specs=[ANY_SPEC] * 3,
        out_specs=VMEM_SPEC,
        out_shape=pltpu.HBM((rank, NV), F32),
        scratch_shapes=[
            pltpu.VMEM((rows, NV), F32),
            pltpu.VMEM((rows, NV), F32),
            pltpu.VMEM((rows, rank), BF16),
            pltpu.VMEM((NV, rank), F32),
            pltpu.SemaphoreType.DMA((3, rows // BLK)),
        ],
        compiler_params=pltpu.CompilerParams(vmem_limit_bytes=12 * MIB),
        name="project",
    )(*in_hbm(x, y, basis))


def list_product(kernel, columns, list_ref, b):
    left = jnp.concatenate([kernel[b, n] for n in range(NBLK)], axis=1)
    right = jnp.concatenate([columns[list_ref[b, n]] for n in range(NBLK)], axis=0)
    return jnp.dot(left, right, preferred_element_type=F32)


def load_patch(slot_ref, chunks, flat, sems):
    rows = chunks[0].shape[0]
    copies = []
    for k, chunk in enumerate(chunks):
        slot = slot_ref[0] ^ (k // 2)
        start = pl.multiple_of(slot * 2 * rows + (k % 2) * rows, rows)
        copies.append(pltpu.make_async_copy(chunk, flat.at[pl.ds(start, rows)], sems.at[k]))
        copies[-1].start()
    return copies


def gather_body(slot_ref, partner_ref, *refs):
    chunks = refs[:8]
    columns_ref, source, gathered, sems = refs[8:]
    for copy in load_patch(slot_ref, chunks, source.reshape(2 * source.shape[0], NV), sems):
        copy.wait()
    unroll = 64

    def gather(step, carry):
        base = step * unroll
        for u in range(unroll):
            gathered[base + u] = source[partner_ref[0, base + u]]
        return carry

    lax.fori_loop(0, source.shape[0] // unroll, gather, 0)
    select = split_matrix()
    flat_out = gathered.reshape(2 * gathered.shape[0], NV)

    def split(block, carry):
        split_block(flat_out, block, columns_ref, select)
        return carry

    lax.fori_loop(0, columns_ref.shape[0], split, 0, unroll=8)


def mirror_columns(slot, partner, chunks):
    patch = partner.shape[1]
    return pl.pallas_call(
        gather_body,
        in_specs=[SMEM_SPEC] * 2 + [ANY_SPEC] * 8,
        out_specs=VMEM_SPEC,
        out_shape=jax.ShapeDtypeStruct((patch // BLK, BLK, 2 * NV), BF16),
        scratch_shapes=[
            pltpu.VMEM((patch, 2, NV), BF16),
            pltpu.VMEM((patch, 2, NV), BF16),
            pltpu.SemaphoreType.DMA((8,)),
        ],
        compiler_params=pltpu.CompilerParams(vmem_limit_bytes=16 * MIB),
        name="mirror_columns",
    )(slot, partner, *in_hbm(*chunks))


def product_body(list_ref, columns_ref, kernel_hbm, out_ref, kernel, sems):
    blocks = kernel.shape[0]

    def load(b):
        return pltpu.make_async_copy(kernel_hbm.at[b], kernel.at[b], sems.at[b])

    for b in range(blocks):
        load(b).start()

    def step(b, carry):
        load(b).wait()
        out_ref[b] = list_product(kernel, columns_ref, list_ref, b)
        return carry

    lax.fori_loop(0, blocks, step, 0)


def mirror_product(indices, columns, kernel):
    blocks = kernel.shape[0]
    return pl.pallas_call(
        product_body,
        in_specs=[SMEM_SPEC, VMEM_SPEC, ANY_SPEC],
        out_specs=VMEM_SPEC,
        out_shape=jax.ShapeDtypeStruct((blocks, BLK, 2 * NV), F32),
        scratch_shapes=[pltpu.VMEM(kernel.shape, BF16), pltpu.SemaphoreType.DMA((blocks,))],
        compiler_params=pltpu.CompilerParams(vmem_limit_bytes=16 * MIB),
        name="mirror_product",
    )(indices, columns, *in_hbm(kernel))


def column_of(row):
    return jnp.broadcast_to(row, (NV, NV)).T


def finish_body(last, slot_ref, list_ref, *refs):
    chunks = refs[:8]
    x_hbm, y_hbm, energy_ref, shift_ref, kernel_hbm, basis_hbm, kept_hbm, other_hbm, mirror_ref = refs[8:17]
    rest = refs[17:]
    if last:
        next_x_hbm, next_y_hbm = rest[:2]
        flat, columns, kernel, basis, x, y, weights, chunk_sems, sems, weight_sems = rest[2:]
    else:
        next_x_hbm, next_y_hbm, low_ref, high_ref, project_ref = rest[:5]
        flat, columns, kernel, basis, x, y, weights, chunk_sems, sems, weight_sems, scratch, total = rest[5:]
    blocks = kernel.shape[0]
    copies = load_patch(slot_ref, chunks, flat, chunk_sems)
    side = weights.shape[0] // 2
    for k, half_hbm in enumerate((kept_hbm, other_hbm)):
        place = pl.ds(pl.multiple_of(((slot_ref[0] ^ k) & 1) * side, side), side)
        copies.append(pltpu.make_async_copy(half_hbm, weights.at[place], weight_sems.at[k]))
        copies[-1].start()

    def load(b, t):
        if t == 0:
            return pltpu.make_async_copy(kernel_hbm.at[b], kernel.at[b], sems.at[0, b])
        source, target = ((basis_hbm, basis), (x_hbm, x), (y_hbm, y))[t - 1]
        part = block_rows(b)
        return pltpu.make_async_copy(source.at[part], target.at[part], sems.at[t, b])

    def save(b, t):
        source, target = ((x, next_x_hbm), (y, next_y_hbm))[t]
        part = block_rows(b)
        return pltpu.make_async_copy(source.at[part], target.at[part], sems.at[2 + t, b])

    for b in range(blocks):
        for t in range(4):
            load(b, t).start()
    for copy in copies:
        copy.wait()
    select = split_matrix()

    def split(block, carry):
        split_block(flat, block, columns, select)
        return carry

    lax.fori_loop(0, columns.shape[0], split, 0, unroll=8)
    shifts = shift_ref[...]
    half = BLK // 2

    def step(b, carry):
        for t in range(4):
            load(b, t).wait()
        part = block_rows(b)
        mirrored = mirror_ref[b]
        exchange = jnp.dot(basis[part, :], weights[...], preferred_element_type=F32)
        direct = list_product(kernel, columns, list_ref, b)
        row = energy_ref[b]
        levels = jnp.concatenate([column_of(row[:, 0:half]), column_of(row[:, half:])], axis=0)
        next_x = x[part, :] + (direct[:, :NV] + mirrored[:, NV:] + exchange) / (levels - shifts)
        next_y = y[part, :] + (direct[:, NV:] + mirrored[:, :NV] + exchange) / (levels + shifts)
        x[part, :] = next_x
        y[part, :] = next_y
        for t in range(2):
            save(b, t).start()
        if not last:
            mixed = interleave(next_x, next_y, scratch)
            place = pl.ds(pl.multiple_of((b % (blocks // 2)) * 2 * BLK, 2 * BLK), 2 * BLK)

            @pl.when(b < blocks // 2)
            def _():
                low_ref[place, :] = mixed

            @pl.when(b >= blocks // 2)
            def _():
                high_ref[place, :] = mixed

            add_projection(total, b == 0, next_x, next_y, basis[part, :])
        return carry

    lax.fori_loop(0, blocks, step, 0)
    if not last:
        store_projection(total, project_ref)
    for b in range(blocks):
        for t in range(2):
            save(b, t).wait()


def finish(last, slot, indices, chunks, x, y, energy, shift, kernel, basis, weights, mirrored):
    rows, rank = basis.shape
    blocks = kernel.shape[0]
    patch = 4 * rows
    out_specs = [ANY_SPEC, ANY_SPEC]
    out_shape = [pltpu.HBM((rows, NV), F32)] * 2
    scratch = [
        pltpu.VMEM((2 * patch, NV), BF16),
        pltpu.VMEM((patch // BLK, BLK, 2 * NV), BF16),
        pltpu.VMEM(kernel.shape, BF16),
        pltpu.VMEM(basis.shape, BF16),
        pltpu.VMEM((rows, NV), F32),
        pltpu.VMEM((rows, NV), F32),
        pltpu.VMEM((rank, NV), BF16),
        pltpu.SemaphoreType.DMA((8,)),
        pltpu.SemaphoreType.DMA((4, blocks)),
        pltpu.SemaphoreType.DMA((2,)),
    ]
    if not last:
        out_specs += [VMEM_SPEC] * 3
        out_shape += [jax.ShapeDtypeStruct((rows, NV), BF16)] * 2 + [pltpu.HBM((rank, NV), F32)]
        scratch += [pltpu.VMEM((2 * BLK, NV), F32), pltpu.VMEM((NV, rank), F32)]

    def body(*refs):
        finish_body(last, *refs)

    return pl.pallas_call(
        body,
        in_specs=[SMEM_SPEC] * 2 + [ANY_SPEC] * 10 + [VMEM_SPEC] * 2 + [ANY_SPEC] * 4 + [VMEM_SPEC],
        out_specs=out_specs,
        out_shape=out_shape,
        scratch_shapes=scratch,
        compiler_params=pltpu.CompilerParams(vmem_limit_bytes=32 * MIB),
        name="finish_last" if last else "finish",
    )(slot, indices, *in_hbm(*chunks, x, y), energy, shift, *in_hbm(kernel, basis, *weights), mirrored)


def half_of(array, index):
    rows = array.shape[0] // 2
    return lax.dynamic_slice_in_dim(array, index * rows, rows, 0)


def total_weights(partial, near, far):
    wide = lax.axis_size("wide")
    plane = wide // 2
    groups = [list(range(plane)), list(range(plane, wide))]
    core = lax.axis_index("narrow") % 2
    rank, vectors = partial.shape
    part = rank // (2 * plane)
    mine = half_of(partial, core) + toggled(half_of(partial, 1 - core), 1)
    pieces = lax.all_to_all(mine.reshape(plane, part, vectors), "wide", 0, 0, axis_index_groups=groups, tiled=True)
    own = jnp.sum(pieces, axis=0)
    others = [toggled(own, mask) for mask in (near, far, near ^ far)]
    final = ((own + others[0]) + (others[1] + others[2])).astype(BF16)
    spread = lax.all_to_all(
        jnp.broadcast_to(final[None], (plane, part, vectors)), "wide", 0, 0, axis_index_groups=groups, tiled=True
    )
    kept = spread.reshape(rank // 2, vectors)
    return kept, toggled(kept, 1)


def on_device(x, y, energy, shift, res_kernel, res_list, cp_kernel, cp_list, partner, basis):
    size = lax.axis_size(AXES)
    narrow = lax.axis_size("narrow")
    near = size // 2
    far = near | (narrow // 2)
    slot = lax.axis_index("narrow").astype(jnp.int32).reshape(1)
    blocks = res_kernel.shape[0]
    levels = energy.reshape(blocks, 1, BLK)
    shifts = shift.reshape(1, NV)
    for app in range(APPS):
        last = app == APPS - 1
        if app == 0:
            low, high = pack(x, y)
            partial = project(x, y, basis)
        far_low = toggled(low, far)
        near_high = toggled(high, near)
        far_high = toggled(high, far)
        near_low = toggled(low, near)
        own = [toggled(low, 1), toggled(high, 1)]
        across = [toggled(far_low, near), toggled(near_high, far)]
        mirror_chunks = [near_low, near_high]
        mirror_chunks += [toggled(c, 1) for c in mirror_chunks]
        mirror_chunks += [far_low, far_high]
        mirror_chunks += [toggled(c, 1) for c in mirror_chunks[4:]]
        own_chunks = [low, high] + own + across + [toggled(c, 1) for c in across]
        weights = total_weights(partial, near, far)
        mirror = mirror_columns(slot, partner, mirror_chunks)
        mirrored = mirror_product(cp_list, mirror, cp_kernel)
        out = finish(
            last, slot, res_list, own_chunks, x, y, levels, shifts, res_kernel, basis, weights, mirrored
        )
        if last:
            return tuple(out)
        x, y, low, high, partial = out


def solution(mesh):
    return jax.shard_map(
        on_device,
        mesh=mesh,
        in_specs=(
            P(AXES, None),
            P(AXES, None),
            P(AXES),
            P(),
            P(AXES, None, None, None),
            P(AXES, None),
            P(AXES, None, None, None),
            P(AXES, None),
            P("wide", None),
            P(AXES, None),
        ),
        out_specs=(P(AXES, None), P(AXES, None)),
        check_vma=False,
    )
```

```python
import jax
import jax.numpy as jnp
from jax import lax
from jax.experimental import pallas as pl
from jax.experimental.pallas import tpu as pltpu
from jax.sharding import PartitionSpec as P


BLK = 256
NV = 128
NBLK = 8
APPS = 2
AXES = ("wide", "narrow")
BF16 = jnp.bfloat16
F32 = jnp.float32
MIB = 1 << 20


VMEM_SPEC = pl.BlockSpec(memory_space=pltpu.VMEM)
SMEM_SPEC = pl.BlockSpec(memory_space=pltpu.SMEM)
ANY_SPEC = pl.BlockSpec(memory_space=pl.ANY)


def toggled(array, mask):
    return lax.ppermute(array, AXES, [(i, i ^ mask) for i in range(lax.axis_size(AXES))])


def interleave(x, y, scratch):
    scratch[pl.ds(0, x.shape[0], stride=2), :] = x
    scratch[pl.ds(1, x.shape[0], stride=2), :] = y
    return scratch[...].astype(BF16)


def in_hbm(*arrays):
    return [pltpu.with_memory_space_constraint(a, pltpu.HBM) for a in arrays]


def block_rows(b, size=BLK):
    return pl.ds(pl.multiple_of(b * size, size), size)


def split_matrix():
    row = lax.broadcasted_iota(jnp.int32, (BLK, BLK), 0)
    col = lax.broadcasted_iota(jnp.int32, (BLK, BLK), 1)
    half = BLK // 2
    hit = (col == 2 * row) | (col == 2 * (row - half) + 1)
    return jnp.where(hit, 1.0, 0.0).astype(F32).astype(BF16)


def split_block(flat, base, block, out, select):
    half = BLK // 2
    pair = jnp.concatenate([flat[pl.ds(base, BLK), :], flat[pl.ds(base + BLK, BLK), :]], axis=1)
    parts = jnp.dot(select, pair, preferred_element_type=F32).astype(BF16)
    out[block, 0:half, 0:NV] = parts[0:half, 0:NV]
    out[block, half:BLK, 0:NV] = parts[0:half, NV:]
    out[block, 0:half, NV:] = parts[half:, 0:NV]
    out[block, half:BLK, NV:] = parts[half:, NV:]


def pack_body(x_hbm, y_hbm, low_ref, high_ref, x, y, scratch, sems):
    size = scratch.shape[0] // 2
    parts = x.shape[0] // size
    loads = []
    for p in range(parts):
        for t, (source, target) in enumerate(((x_hbm, x), (y_hbm, y))):
            rows = pl.ds(p * size, size)
            loads.append(pltpu.make_async_copy(source.at[rows], target.at[rows], sems.at[2 * p + t]))
            loads[-1].start()
    for p in range(parts):
        loads[2 * p].wait()
        loads[2 * p + 1].wait()
        rows = pl.ds(p * size, size)
        out, place = (low_ref, p) if p < parts // 2 else (high_ref, p - parts // 2)
        out[pl.ds(place * 2 * size, 2 * size), :] = interleave(x[rows, :], y[rows, :], scratch)


def pack(x, y):
    rows = x.shape[0]
    parts = 4
    return pl.pallas_call(
        pack_body,
        in_specs=[ANY_SPEC, ANY_SPEC],
        out_specs=[VMEM_SPEC, VMEM_SPEC],
        out_shape=[jax.ShapeDtypeStruct((rows, NV), BF16)] * 2,
        scratch_shapes=[
            pltpu.VMEM((rows, NV), F32),
            pltpu.VMEM((rows, NV), F32),
            pltpu.VMEM((2 * rows // parts, NV), F32),
            pltpu.SemaphoreType.DMA((2 * parts,)),
        ],
        compiler_params=pltpu.CompilerParams(vmem_limit_bytes=8 * MIB),
        name="pack",
    )(*in_hbm(x, y))


def project_body(x_hbm, y_hbm, basis_hbm, out_ref, x, y, basis, summed, sems):
    copies = []
    for t, (source, target) in enumerate(((x_hbm, x), (y_hbm, y), (basis_hbm, basis))):
        copies.append(pltpu.make_async_copy(source, target, sems.at[t]))
        copies[-1].start()
    copies[0].wait()
    copies[1].wait()
    rows = x.shape[0]
    for b in range(rows // BLK):
        part = pl.ds(b * BLK, BLK)
        summed[:, b * BLK : (b + 1) * BLK] = (x[part, :] + y[part, :]).T.astype(BF16)
    copies[2].wait()
    rank = basis.shape[1]
    wide = 2 * BLK
    for r in range(rank // wide):
        value = jnp.dot(summed[...], basis[:, r * wide : (r + 1) * wide], preferred_element_type=F32)
        for q in range(wide // NV):
            row = r * wide + q * NV
            out_ref[row : row + NV, :] = value[:, q * NV : (q + 1) * NV].T


def project(x, y, basis):
    rows, rank = basis.shape
    return pl.pallas_call(
        project_body,
        in_specs=[ANY_SPEC] * 3,
        out_specs=VMEM_SPEC,
        out_shape=pltpu.HBM((rank, NV), F32),
        scratch_shapes=[
            pltpu.VMEM((rows, NV), F32),
            pltpu.VMEM((rows, NV), F32),
            pltpu.VMEM((rows, rank), BF16),
            pltpu.VMEM((NV, rows), BF16),
            pltpu.SemaphoreType.DMA((3,)),
        ],
        compiler_params=pltpu.CompilerParams(vmem_limit_bytes=12 * MIB),
        name="project",
    )(*in_hbm(x, y, basis))


def list_product(kernel, columns, list_ref, b):
    left = jnp.concatenate([kernel[b, n] for n in range(NBLK)], axis=1)
    right = jnp.concatenate([columns[list_ref[b, n]] for n in range(NBLK)], axis=0)
    return jnp.dot(left, right, preferred_element_type=F32)


def load_patch(slot, chunks, flat, sems):
    rows = chunks[0].shape[0]
    copies = []
    for k, chunk in enumerate(chunks):
        start = pl.multiple_of((slot ^ (k // 2)) * 2 * rows + (k % 2) * rows, rows)
        copies.append(pltpu.make_async_copy(chunk, flat.at[pl.ds(start, rows)], sems.at[k]))
        copies[-1].start()
    return copies


def split_all(flat, first, out, select):
    def split(block, carry):
        split_block(flat, pl.multiple_of(block * 2 * BLK, 2 * BLK), first + block, out, select)
        return carry

    lax.fori_loop(0, flat.shape[0] // (2 * BLK), split, 0, unroll=8)


def own_body(slot_ref, *refs):
    chunks = refs[:4]
    out_ref, flat, sems = refs[4:]
    copies = load_patch(slot_ref[0] & 1, chunks, flat, sems)
    select = split_matrix()
    for copy in copies:
        copy.wait()
    split_all(flat, 0, out_ref, select)


def own_columns(slot, chunks):
    rows = chunks[0].shape[0]
    return pl.pallas_call(
        own_body,
        in_specs=[SMEM_SPEC] + [ANY_SPEC] * 4,
        out_specs=VMEM_SPEC,
        out_shape=pltpu.HBM((2 * rows // BLK, BLK, 2 * NV), BF16),
        scratch_shapes=[pltpu.VMEM((4 * rows, NV), BF16), pltpu.SemaphoreType.DMA((4,))],
        compiler_params=pltpu.CompilerParams(vmem_limit_bytes=8 * MIB),
        name="own_columns",
    )(slot, *in_hbm(*chunks))


def mirror_body(slot_ref, partner_ref, list_ref, *refs):
    chunks = refs[:8]
    kernel_hbm, out_ref, source, gathered, columns, kernel, sems, kernel_sems = refs[8:]
    copies = load_patch(slot_ref[0], chunks, source.reshape(2 * source.shape[0], NV), sems)
    blocks = kernel.shape[0]
    loads = [pltpu.make_async_copy(kernel_hbm.at[b], kernel.at[b], kernel_sems.at[b]) for b in range(blocks)]
    for load in loads:
        load.start()
    select = split_matrix()
    for copy in copies:
        copy.wait()
    unroll = 128

    def gather(step, carry):
        base = step * unroll
        for u in range(unroll):
            gathered[base + u] = source[partner_ref[0, base + u]]
        return carry

    lax.fori_loop(0, source.shape[0] // unroll, gather, 0)
    split_all(gathered.reshape(2 * gathered.shape[0], NV), 0, columns, select)
    for load in loads:
        load.wait()

    def product(b, carry):
        out_ref[b] = list_product(kernel, columns, list_ref, b)
        return carry

    lax.fori_loop(0, blocks, product, 0, unroll=2)


def mirror_product(slot, partner, indices, chunks, kernel):
    patch = partner.shape[1]
    blocks = kernel.shape[0]
    return pl.pallas_call(
        mirror_body,
        in_specs=[SMEM_SPEC] * 3 + [ANY_SPEC] * 9,
        out_specs=VMEM_SPEC,
        out_shape=jax.ShapeDtypeStruct((blocks, BLK, 2 * NV), F32),
        scratch_shapes=[
            pltpu.VMEM((patch, 2, NV), BF16),
            pltpu.VMEM((patch, 2, NV), BF16),
            pltpu.VMEM((patch // BLK, BLK, 2 * NV), BF16),
            pltpu.VMEM(kernel.shape, BF16),
            pltpu.SemaphoreType.DMA((8,)),
            pltpu.SemaphoreType.DMA((blocks,)),
        ],
        compiler_params=pltpu.CompilerParams(vmem_limit_bytes=24 * MIB),
        name="mirror_product",
    )(slot, partner, indices, *in_hbm(*chunks, kernel))


def column_of(row):
    return jnp.broadcast_to(row, (NV, NV)).T


def finish_body(last, slot_ref, list_ref, *refs):
    chunks = refs[:4]
    own_hbm, x_hbm, y_hbm, energy_ref, shift_ref, kernel_hbm, basis_hbm, weight_ref, mirror_ref = refs[4:13]
    rest = refs[13:]
    if last:
        next_x_hbm, next_y_hbm = rest[:2]
        rest = rest[2:]
    else:
        next_x_hbm, next_y_hbm, low_ref, high_ref = rest[:4]
        rest = rest[4:]
    flat, columns, kernel, basis, x, y, levels, scratch, chunk_sems, sems, save_sems = rest
    blocks = kernel.shape[0]
    core = slot_ref[0] & 1
    copies = load_patch(core, chunks, flat, chunk_sems)
    count = own_hbm.shape[0]
    own_first = (slot_ref[0] // 2) * count
    extra = [pltpu.make_async_copy(own_hbm, columns.at[pl.ds(own_first, count)], chunk_sems.at[4])]
    for copy in extra:
        copy.start()

    def load(b, t):
        if t == 0:
            return pltpu.make_async_copy(kernel_hbm.at[b], kernel.at[b], sems.at[0, b])
        source, target = ((basis_hbm, basis), (x_hbm, x), (y_hbm, y))[t - 1]
        part = block_rows(b)
        return pltpu.make_async_copy(source.at[part], target.at[part], sems.at[t, b])

    def save(b, t):
        source, target = ((x, next_x_hbm), (y, next_y_hbm))[t]
        part = block_rows(b)
        return pltpu.make_async_copy(source.at[part], target.at[part], save_sems.at[t, b])

    for b in range(blocks):
        for t in range(4):
            load(b, t).start()
    half = BLK // 2
    for b in range(blocks):
        row = energy_ref[b]
        levels[b * BLK : b * BLK + half, :] = column_of(row[:, 0:half])
        levels[b * BLK + half : (b + 1) * BLK, :] = column_of(row[:, half:])
    for copy in copies:
        copy.wait()
    split_all(flat, (1 - slot_ref[0] // 2) * count, columns, split_matrix())
    for copy in extra:
        copy.wait()
    for b in range(blocks):
        for t in range(4):
            load(b, t).wait()
    shifts = shift_ref[...]

    def step(b):
        part = block_rows(b)
        mirrored = mirror_ref[b]
        exchange = jnp.dot(basis[part, :], weight_ref[...], preferred_element_type=F32)
        direct = list_product(kernel, columns, list_ref, b)
        level = levels[part, :]
        next_x = x[part, :] + (direct[:, :NV] + mirrored[:, NV:] + exchange) / (level - shifts)
        next_y = y[part, :] + (direct[:, NV:] + mirrored[:, :NV] + exchange) / (level + shifts)
        x[part, :] = next_x
        y[part, :] = next_y
        for t in range(2):
            save(b, t).start()
        return (next_x, next_y)

    if last:
        lax.fori_loop(0, blocks, lambda b, carry: (step(b), carry)[1], 0, unroll=2)
    else:
        for place, out_ref in enumerate((low_ref, high_ref)):
            base = place * (blocks // 2)

            def pair(b, carry):
                next_x, next_y = step(base + b)
                out_ref[block_rows(b, 2 * BLK), :] = interleave(next_x, next_y, scratch.at[b % 2])
                return carry

            lax.fori_loop(0, blocks // 2, pair, 0, unroll=2)
    for b in range(blocks):
        for t in range(2):
            save(b, t).wait()


def finish(last, slot, indices, chunks, own, x, y, energy, shift, kernel, basis, weights, mirrored):
    rows, _ = basis.shape
    blocks = kernel.shape[0]
    patch = 4 * rows
    out_specs = [ANY_SPEC, ANY_SPEC]
    out_shape = [pltpu.HBM((rows, NV), F32)] * 2
    if not last:
        out_specs += [VMEM_SPEC] * 2
        out_shape += [jax.ShapeDtypeStruct((rows, NV), BF16)] * 2

    def body(*refs):
        finish_body(last, *refs)

    return pl.pallas_call(
        body,
        in_specs=[SMEM_SPEC] * 2 + [ANY_SPEC] * 7 + [VMEM_SPEC] * 2 + [ANY_SPEC] * 2 + [VMEM_SPEC] * 2,
        out_specs=out_specs,
        out_shape=out_shape,
        scratch_shapes=[
            pltpu.VMEM((patch, NV), BF16),
            pltpu.VMEM((patch // BLK, BLK, 2 * NV), BF16),
            pltpu.VMEM(kernel.shape, BF16),
            pltpu.VMEM(basis.shape, BF16),
            pltpu.VMEM((rows, NV), F32),
            pltpu.VMEM((rows, NV), F32),
            pltpu.VMEM((rows, NV), F32),
            pltpu.VMEM((2, 2 * BLK, NV), F32),
            pltpu.SemaphoreType.DMA((8,)),
            pltpu.SemaphoreType.DMA((4, blocks)),
            pltpu.SemaphoreType.DMA((2, blocks)),
        ],
        compiler_params=pltpu.CompilerParams(vmem_limit_bytes=32 * MIB),
        name="finish_last" if last else "finish",
    )(slot, indices, *in_hbm(*chunks, own, x, y), energy, shift, *in_hbm(kernel, basis), weights, mirrored)


def total_weights(partial):
    size = lax.axis_size(AXES)
    rank, vectors = partial.shape
    part = rank // size
    pieces = lax.all_to_all(partial.reshape(size, part, vectors), AXES, 0, 0, tiled=True)
    own = jnp.sum(pieces.astype(F32), axis=0).astype(BF16)
    spread = lax.all_to_all(jnp.broadcast_to(own[None], (size, part, vectors)), AXES, 0, 0, tiled=True)
    return spread.reshape(rank, vectors)


def on_device(x, y, energy, shift, res_kernel, res_list, cp_kernel, cp_list, partner, basis):
    size = lax.axis_size(AXES)
    narrow = lax.axis_size("narrow")
    near = size // 2
    far = near | (narrow // 2)
    slot = lax.axis_index("narrow").astype(jnp.int32).reshape(1)
    blocks = res_kernel.shape[0]
    levels = energy.reshape(blocks, 1, BLK)
    shifts = shift.reshape(1, NV)
    for app in range(APPS):
        last = app == APPS - 1
        if app == 0:
            low, high = pack(x, y)
        far_low = toggled(low, far)
        near_high = toggled(high, near)
        weights = total_weights(project(x, y, basis))
        far_high = toggled(high, far)
        near_low = toggled(low, near)
        own = [toggled(low, 1), toggled(high, 1)]
        across = [toggled(far_low, near), toggled(near_high, far)]
        near_swap = [toggled(near_low, 1), toggled(near_high, 1)]
        far_swap = [toggled(far_low, 1), toggled(far_high, 1)]
        mirror_chunks = [near_low, near_high] + near_swap + [far_low, far_high] + far_swap
        own_half = own_columns(slot, [low, high] + own)
        across += [toggled(c, 1) for c in across]
        mirrored = mirror_product(slot, partner, cp_list, mirror_chunks, cp_kernel)
        out = finish(last, slot, res_list, across, own_half, x, y, levels, shifts, res_kernel, basis, weights, mirrored)
        if last:
            return tuple(out)
        x, y, low, high = out


def solution(mesh):
    return jax.shard_map(
        on_device,
        mesh=mesh,
        in_specs=(
            P(AXES, None),
            P(AXES, None),
            P(AXES),
            P(),
            P(AXES, None, None, None),
            P(AXES, None),
            P(AXES, None, None, None),
            P(AXES, None),
            P("wide", None),
            P(AXES, None),
        ),
        out_specs=(P(AXES, None), P(AXES, None)),
        check_vma=False,
    )
```

```python
import jax
import jax.numpy as jnp
from jax import lax
from jax.experimental import pallas as pl
from jax.experimental.pallas import tpu as pltpu
from jax.sharding import PartitionSpec as P


BLK = 256
NV = 128
NBLK = 8
APPS = 2
AXES = ("wide", "narrow")
BF16 = jnp.bfloat16
F32 = jnp.float32
MIB = 1 << 20


VMEM_SPEC = pl.BlockSpec(memory_space=pltpu.VMEM)
SMEM_SPEC = pl.BlockSpec(memory_space=pltpu.SMEM)
ANY_SPEC = pl.BlockSpec(memory_space=pl.ANY)


def toggled(array, mask):
    return lax.ppermute(array, AXES, [(i, i ^ mask) for i in range(lax.axis_size(AXES))])


def interleave(x, y, scratch):
    scratch[pl.ds(0, x.shape[0], stride=2), :] = x
    scratch[pl.ds(1, x.shape[0], stride=2), :] = y
    return scratch[...].astype(BF16)


def in_hbm(*arrays):
    return [pltpu.with_memory_space_constraint(a, pltpu.HBM) for a in arrays]


def block_rows(b, size=BLK):
    return pl.ds(pl.multiple_of(b * size, size), size)


def split_matrix():
    row = lax.broadcasted_iota(jnp.int32, (BLK, BLK), 0)
    col = lax.broadcasted_iota(jnp.int32, (BLK, BLK), 1)
    half = BLK // 2
    hit = (col == 2 * row) | (col == 2 * (row - half) + 1)
    return jnp.where(hit, 1.0, 0.0).astype(F32).astype(BF16)


def split_block(flat, base, block, out, select):
    half = BLK // 2
    pair = jnp.concatenate([flat[pl.ds(base, BLK), :], flat[pl.ds(base + BLK, BLK), :]], axis=1)
    parts = jnp.dot(select, pair, preferred_element_type=F32).astype(BF16)
    out[block, 0:half, 0:NV] = parts[0:half, 0:NV]
    out[block, half:BLK, 0:NV] = parts[0:half, NV:]
    out[block, 0:half, NV:] = parts[half:, 0:NV]
    out[block, half:BLK, NV:] = parts[half:, NV:]


def pack_body(x_hbm, y_hbm, low_ref, high_ref, x, y, scratch, sems):
    size = scratch.shape[0] // 2
    parts = x.shape[0] // size
    loads = []
    for p in range(parts):
        for t, (source, target) in enumerate(((x_hbm, x), (y_hbm, y))):
            rows = pl.ds(p * size, size)
            loads.append(pltpu.make_async_copy(source.at[rows], target.at[rows], sems.at[2 * p + t]))
            loads[-1].start()
    for p in range(parts):
        loads[2 * p].wait()
        loads[2 * p + 1].wait()
        rows = pl.ds(p * size, size)
        out, place = (low_ref, p) if p < parts // 2 else (high_ref, p - parts // 2)
        out[pl.ds(place * 2 * size, 2 * size), :] = interleave(x[rows, :], y[rows, :], scratch)


def pack(x, y):
    rows = x.shape[0]
    parts = 4
    return pl.pallas_call(
        pack_body,
        in_specs=[ANY_SPEC, ANY_SPEC],
        out_specs=[VMEM_SPEC, VMEM_SPEC],
        out_shape=[jax.ShapeDtypeStruct((rows, NV), BF16)] * 2,
        scratch_shapes=[
            pltpu.VMEM((rows, NV), F32),
            pltpu.VMEM((rows, NV), F32),
            pltpu.VMEM((2 * rows // parts, NV), F32),
            pltpu.SemaphoreType.DMA((2 * parts,)),
        ],
        compiler_params=pltpu.CompilerParams(vmem_limit_bytes=8 * MIB),
        name="pack",
    )(*in_hbm(x, y))


def store_projection(summed, basis, out_ref):
    rank = basis.shape[1]
    wide = 2 * BLK
    for r in range(rank // wide):
        value = jnp.dot(summed[...], basis[:, r * wide : (r + 1) * wide], preferred_element_type=F32)
        for q in range(wide // NV):
            row = r * wide + q * NV
            out_ref[row : row + NV, :] = value[:, q * NV : (q + 1) * NV].T


def add_vectors(x, y):
    return (x + y).T.astype(BF16)


def project_body(x_hbm, y_hbm, basis_hbm, out_ref, x, y, basis, summed, sems):
    copies = []
    for t, (source, target) in enumerate(((x_hbm, x), (y_hbm, y), (basis_hbm, basis))):
        copies.append(pltpu.make_async_copy(source, target, sems.at[t]))
        copies[-1].start()
    copies[0].wait()
    copies[1].wait()
    rows = x.shape[0]
    for b in range(rows // BLK):
        part = pl.ds(b * BLK, BLK)
        summed[:, b * BLK : (b + 1) * BLK] = add_vectors(x[part, :], y[part, :])
    copies[2].wait()
    store_projection(summed, basis, out_ref)


def project(x, y, basis):
    rows, rank = basis.shape
    return pl.pallas_call(
        project_body,
        in_specs=[ANY_SPEC] * 3,
        out_specs=VMEM_SPEC,
        out_shape=pltpu.HBM((rank, NV), F32),
        scratch_shapes=[
            pltpu.VMEM((rows, NV), F32),
            pltpu.VMEM((rows, NV), F32),
            pltpu.VMEM((rows, rank), BF16),
            pltpu.VMEM((NV, rows), BF16),
            pltpu.SemaphoreType.DMA((3,)),
        ],
        compiler_params=pltpu.CompilerParams(vmem_limit_bytes=12 * MIB),
        name="project",
    )(*in_hbm(x, y, basis))


def list_product(kernel, columns, list_ref, b):
    left = jnp.concatenate([kernel[b, n] for n in range(NBLK)], axis=1)
    right = jnp.concatenate([columns[list_ref[b, n]] for n in range(NBLK)], axis=0)
    return jnp.dot(left, right, preferred_element_type=F32)


def load_patch(slot, chunks, flat, sems):
    rows = chunks[0].shape[0]
    copies = []
    for k, chunk in enumerate(chunks):
        start = pl.multiple_of((slot ^ (k // 2)) * 2 * rows + (k % 2) * rows, rows)
        copies.append(pltpu.make_async_copy(chunk, flat.at[pl.ds(start, rows)], sems.at[k]))
        copies[-1].start()
    return copies


def split_all(flat, first, out, select):
    def split(block, carry):
        split_block(flat, pl.multiple_of(block * 2 * BLK, 2 * BLK), first + block, out, select)
        return carry

    lax.fori_loop(0, flat.shape[0] // (2 * BLK), split, 0, unroll=16)


def own_body(slot_ref, *refs):
    chunks = refs[:4]
    out_ref, flat, sems = refs[4:]
    copies = load_patch(slot_ref[0] & 1, chunks, flat, sems)
    select = split_matrix()
    for copy in copies:
        copy.wait()
    split_all(flat, 0, out_ref, select)


def own_columns(slot, chunks):
    rows = chunks[0].shape[0]
    return pl.pallas_call(
        own_body,
        in_specs=[SMEM_SPEC] + [ANY_SPEC] * 4,
        out_specs=VMEM_SPEC,
        out_shape=pltpu.HBM((2 * rows // BLK, BLK, 2 * NV), BF16),
        scratch_shapes=[pltpu.VMEM((4 * rows, NV), BF16), pltpu.SemaphoreType.DMA((4,))],
        compiler_params=pltpu.CompilerParams(vmem_limit_bytes=8 * MIB),
        name="own_columns",
    )(slot, *chunks)


def mirror_body(slot_ref, partner_ref, list_ref, *refs):
    chunks = refs[:8]
    kernel_hbm, out_ref, source, gathered, columns, kernel, sems, kernel_sems = refs[8:]
    copies = load_patch(slot_ref[0], chunks, source.reshape(2 * source.shape[0], NV), sems)
    blocks = kernel.shape[0]
    loads = [pltpu.make_async_copy(kernel_hbm.at[b], kernel.at[b], kernel_sems.at[b]) for b in range(blocks)]
    select = split_matrix()
    for copy in copies:
        copy.wait()
    for load in loads:
        load.start()
    unroll = 128

    def gather(step, carry):
        base = step * unroll
        for u in range(unroll):
            gathered[base + u] = source[partner_ref[0, base + u]]
        return carry

    lax.fori_loop(0, source.shape[0] // unroll, gather, 0)
    split_all(gathered.reshape(2 * gathered.shape[0], NV), 0, columns, select)
    for load in loads:
        load.wait()

    def product(b, carry):
        out_ref[b] = list_product(kernel, columns, list_ref, b)
        return carry

    lax.fori_loop(0, blocks, product, 0, unroll=4)


def mirror_product(slot, partner, indices, chunks, kernel):
    patch = partner.shape[1]
    blocks = kernel.shape[0]
    return pl.pallas_call(
        mirror_body,
        in_specs=[SMEM_SPEC] * 3 + [ANY_SPEC] * 9,
        out_specs=VMEM_SPEC,
        out_shape=jax.ShapeDtypeStruct((blocks, BLK, 2 * NV), F32),
        scratch_shapes=[
            pltpu.VMEM((patch, 2, NV), BF16),
            pltpu.VMEM((patch, 2, NV), BF16),
            pltpu.VMEM((patch // BLK, BLK, 2 * NV), BF16),
            pltpu.VMEM(kernel.shape, BF16),
            pltpu.SemaphoreType.DMA((8,)),
            pltpu.SemaphoreType.DMA((blocks,)),
        ],
        compiler_params=pltpu.CompilerParams(vmem_limit_bytes=24 * MIB),
        name="mirror_product",
    )(slot, partner, indices, *in_hbm(*chunks, kernel))


def column_of(row):
    return jnp.broadcast_to(row, (NV, NV)).T


def finish_body(last, slot_ref, list_ref, *refs):
    chunks = refs[:4]
    own_hbm, x_hbm, y_hbm, energy_ref, shift_ref, kernel_hbm, basis_hbm, weight_ref, mirror_ref = refs[4:13]
    rest = refs[13:]
    if last:
        next_x_hbm, next_y_hbm = rest[:2]
        rest = rest[2:]
    else:
        next_x_hbm, next_y_hbm, low_ref, high_ref, project_ref = rest[:5]
        rest = rest[5:]
    flat, columns, kernel, basis, x, y, levels, scratch, summed, chunk_sems, sems, save_sems = rest
    blocks = kernel.shape[0]
    core = slot_ref[0] & 1
    copies = load_patch(core, chunks, flat, chunk_sems)
    count = own_hbm.shape[0]
    own_first = (slot_ref[0] // 2) * count
    extra = [pltpu.make_async_copy(own_hbm, columns.at[pl.ds(own_first, count)], chunk_sems.at[4])]
    for copy in extra:
        copy.start()

    def load(b, t):
        if t == 0:
            return pltpu.make_async_copy(kernel_hbm.at[b], kernel.at[b], sems.at[0, b])
        source, target = ((basis_hbm, basis), (x_hbm, x), (y_hbm, y))[t - 1]
        part = block_rows(b)
        return pltpu.make_async_copy(source.at[part], target.at[part], sems.at[t, b])

    def save(b, t):
        source, target = ((x, next_x_hbm), (y, next_y_hbm))[t]
        part = block_rows(b)
        return pltpu.make_async_copy(source.at[part], target.at[part], save_sems.at[t, b])

    half = BLK // 2
    for b in range(blocks):
        row = energy_ref[b]
        levels[b * BLK : b * BLK + half, :] = column_of(row[:, 0:half])
        levels[b * BLK + half : (b + 1) * BLK, :] = column_of(row[:, half:])
    for copy in copies:
        copy.wait()
    for b in range(blocks):
        for t in range(4):
            load(b, t).start()
    split_all(flat, (1 - slot_ref[0] // 2) * count, columns, split_matrix())
    for copy in extra:
        copy.wait()
    shifts = shift_ref[...]
    for b in range(blocks):
        for t in range(4):
            load(b, t).wait()
        part = pl.ds(b * BLK, BLK)
        mirrored = mirror_ref[b]
        exchange = jnp.dot(basis[part, :], weight_ref[...], preferred_element_type=F32)
        direct = list_product(kernel, columns, list_ref, b)
        level = levels[part, :]
        next_x = x[part, :] + (direct[:, :NV] + mirrored[:, NV:] + exchange) / (level - shifts)
        next_y = y[part, :] + (direct[:, NV:] + mirrored[:, :NV] + exchange) / (level + shifts)
        x[part, :] = next_x
        y[part, :] = next_y
        for t in range(2):
            save(b, t).start()
        if not last:
            out_ref, place = (low_ref, b) if b < blocks // 2 else (high_ref, b - blocks // 2)
            out_ref[pl.ds(place * 2 * BLK, 2 * BLK), :] = interleave(next_x, next_y, scratch.at[b % 2])
            summed[:, b * BLK : (b + 1) * BLK] = add_vectors(next_x, next_y)
    if not last:
        store_projection(summed, basis, project_ref)
    for b in range(blocks):
        for t in range(2):
            save(b, t).wait()


def finish(last, slot, indices, chunks, own, x, y, energy, shift, kernel, basis, weights, mirrored):
    rows, rank = basis.shape
    blocks = kernel.shape[0]
    patch = 4 * rows
    out_specs = [ANY_SPEC, ANY_SPEC]
    out_shape = [pltpu.HBM((rows, NV), F32)] * 2
    if not last:
        out_specs += [VMEM_SPEC] * 3
        out_shape += [jax.ShapeDtypeStruct((rows, NV), BF16)] * 2 + [pltpu.HBM((rank, NV), F32)]

    def body(*refs):
        finish_body(last, *refs)

    return pl.pallas_call(
        body,
        in_specs=[SMEM_SPEC] * 2 + [ANY_SPEC] * 7 + [VMEM_SPEC] * 2 + [ANY_SPEC] * 2 + [VMEM_SPEC] * 2,
        out_specs=out_specs,
        out_shape=out_shape,
        scratch_shapes=[
            pltpu.VMEM((patch, NV), BF16),
            pltpu.VMEM((patch // BLK, BLK, 2 * NV), BF16),
            pltpu.VMEM(kernel.shape, BF16),
            pltpu.VMEM(basis.shape, BF16),
            pltpu.VMEM((rows, NV), F32),
            pltpu.VMEM((rows, NV), F32),
            pltpu.VMEM((rows, NV), F32),
            pltpu.VMEM((2, 2 * BLK, NV), F32),
            pltpu.VMEM((NV, rows), BF16),
            pltpu.SemaphoreType.DMA((8,)),
            pltpu.SemaphoreType.DMA((4, blocks)),
            pltpu.SemaphoreType.DMA((2, blocks)),
        ],
        compiler_params=pltpu.CompilerParams(vmem_limit_bytes=32 * MIB),
        name="finish_last" if last else "finish",
    )(slot, indices, *in_hbm(*chunks, own, x, y), energy, shift, *in_hbm(kernel, basis), weights, mirrored)


def total_weights(partial):
    size = lax.axis_size(AXES)
    rank, vectors = partial.shape
    part = rank // size
    pieces = lax.all_to_all(partial.reshape(size, part, vectors), AXES, 0, 0, tiled=True)
    own = jnp.sum(pieces.astype(F32), axis=0).astype(BF16)
    spread = lax.all_to_all(jnp.broadcast_to(own[None], (size, part, vectors)), AXES, 0, 0, tiled=True)
    return spread.reshape(rank, vectors)


def on_device(x, y, energy, shift, res_kernel, res_list, cp_kernel, cp_list, partner, basis):
    size = lax.axis_size(AXES)
    narrow = lax.axis_size("narrow")
    near = size // 2
    far = near | (narrow // 2)
    slot = lax.axis_index("narrow").astype(jnp.int32).reshape(1)
    blocks = res_kernel.shape[0]
    levels = energy.reshape(blocks, 1, BLK)
    shifts = shift.reshape(1, NV)
    for app in range(APPS):
        last = app == APPS - 1
        if app == 0:
            low, high = pack(x, y)
            partial = project(x, y, basis)
        far_low = toggled(low, far)
        near_high = toggled(high, near)
        weights = total_weights(partial)
        far_high = toggled(high, far)
        near_low = toggled(low, near)
        own = [toggled(low, 1), toggled(high, 1)]
        across = [toggled(far_low, near), toggled(near_high, far)]
        near_swap = [toggled(near_low, 1), toggled(near_high, 1)]
        far_swap = [toggled(far_low, 1), toggled(far_high, 1)]
        mirror_chunks = [near_low, near_high] + near_swap + [far_low, far_high] + far_swap
        own_half = own_columns(slot, [low, high] + own)
        across += [toggled(c, 1) for c in across]
        mirrored = mirror_product(slot, partner, cp_list, mirror_chunks, cp_kernel)
        out = finish(last, slot, res_list, across, own_half, x, y, levels, shifts, res_kernel, basis, weights, mirrored)
        if last:
            return tuple(out)
        x, y, low, high, partial = out


def solution(mesh):
    return jax.shard_map(
        on_device,
        mesh=mesh,
        in_specs=(
            P(AXES, None),
            P(AXES, None),
            P(AXES),
            P(),
            P(AXES, None, None, None),
            P(AXES, None),
            P(AXES, None, None, None),
            P(AXES, None),
            P("wide", None),
            P(AXES, None),
        ),
        out_specs=(P(AXES, None), P(AXES, None)),
        check_vma=False,
    )
```

```python
import jax
import jax.numpy as jnp
from jax import lax
from jax.experimental import pallas as pl
from jax.experimental.pallas import tpu as pltpu
from jax.sharding import PartitionSpec as P


BLK = 256
NV = 128
NBLK = 8
APPS = 2
AXES = ("wide", "narrow")
BF16 = jnp.bfloat16
F32 = jnp.float32
MIB = 1 << 20


VMEM_SPEC = pl.BlockSpec(memory_space=pltpu.VMEM)
SMEM_SPEC = pl.BlockSpec(memory_space=pltpu.SMEM)
ANY_SPEC = pl.BlockSpec(memory_space=pl.ANY)


def toggled(array, mask):
    return lax.ppermute(array, AXES, [(i, i ^ mask) for i in range(lax.axis_size(AXES))])


def interleave(x, y, scratch):
    scratch[pl.ds(0, x.shape[0], stride=2), :] = x
    scratch[pl.ds(1, x.shape[0], stride=2), :] = y
    return scratch[...].astype(BF16)


def in_hbm(*arrays):
    return [pltpu.with_memory_space_constraint(a, pltpu.HBM) for a in arrays]


def block_rows(b, size=BLK):
    return pl.ds(pl.multiple_of(b * size, size), size)


def split_matrix():
    row = lax.broadcasted_iota(jnp.int32, (BLK, BLK), 0)
    col = lax.broadcasted_iota(jnp.int32, (BLK, BLK), 1)
    half = BLK // 2
    hit = (col == 2 * row) | (col == 2 * (row - half) + 1)
    return jnp.where(hit, 1.0, 0.0).astype(F32).astype(BF16)


def split_block(flat, base, block, out, select):
    half = BLK // 2
    pair = jnp.concatenate([flat[pl.ds(base, BLK), :], flat[pl.ds(base + BLK, BLK), :]], axis=1)
    parts = jnp.dot(select, pair, preferred_element_type=F32).astype(BF16)
    out[block, 0:half, 0:NV] = parts[0:half, 0:NV]
    out[block, half:BLK, 0:NV] = parts[0:half, NV:]
    out[block, 0:half, NV:] = parts[half:, 0:NV]
    out[block, half:BLK, NV:] = parts[half:, NV:]


def pack_body(x_hbm, y_hbm, low_ref, high_ref, x, y, scratch, sems):
    size = scratch.shape[0] // 2
    parts = x.shape[0] // size
    loads = []
    for p in range(parts):
        for t, (source, target) in enumerate(((x_hbm, x), (y_hbm, y))):
            rows = pl.ds(p * size, size)
            loads.append(pltpu.make_async_copy(source.at[rows], target.at[rows], sems.at[2 * p + t]))
            loads[-1].start()
    for p in range(parts):
        loads[2 * p].wait()
        loads[2 * p + 1].wait()
        rows = pl.ds(p * size, size)
        out, place = (low_ref, p) if p < parts // 2 else (high_ref, p - parts // 2)
        out[pl.ds(place * 2 * size, 2 * size), :] = interleave(x[rows, :], y[rows, :], scratch)


def pack(x, y):
    rows = x.shape[0]
    parts = 4
    return pl.pallas_call(
        pack_body,
        in_specs=[ANY_SPEC, ANY_SPEC],
        out_specs=[VMEM_SPEC, VMEM_SPEC],
        out_shape=[jax.ShapeDtypeStruct((rows, NV), BF16)] * 2,
        scratch_shapes=[
            pltpu.VMEM((rows, NV), F32),
            pltpu.VMEM((rows, NV), F32),
            pltpu.VMEM((2 * rows // parts, NV), F32),
            pltpu.SemaphoreType.DMA((2 * parts,)),
        ],
        compiler_params=pltpu.CompilerParams(vmem_limit_bytes=8 * MIB),
        name="pack",
    )(*in_hbm(x, y))


def store_projection(summed, basis, out_ref):
    rank = basis.shape[1]
    wide = 2 * BLK
    for r in range(rank // wide):
        value = jnp.dot(summed[...], basis[:, r * wide : (r + 1) * wide], preferred_element_type=F32)
        for q in range(wide // NV):
            row = r * wide + q * NV
            out_ref[row : row + NV, :] = value[:, q * NV : (q + 1) * NV].T


def add_vectors(x, y):
    return (x + y).T.astype(BF16)


def project_body(x_hbm, y_hbm, basis_hbm, out_ref, x, y, basis, summed, sems):
    copies = []
    for t, (source, target) in enumerate(((x_hbm, x), (y_hbm, y), (basis_hbm, basis))):
        copies.append(pltpu.make_async_copy(source, target, sems.at[t]))
        copies[-1].start()
    copies[0].wait()
    copies[1].wait()
    rows = x.shape[0]
    for b in range(rows // BLK):
        part = pl.ds(b * BLK, BLK)
        summed[:, b * BLK : (b + 1) * BLK] = add_vectors(x[part, :], y[part, :])
    copies[2].wait()
    store_projection(summed, basis, out_ref)


def project(x, y, basis):
    rows, rank = basis.shape
    return pl.pallas_call(
        project_body,
        in_specs=[ANY_SPEC] * 3,
        out_specs=VMEM_SPEC,
        out_shape=pltpu.HBM((rank, NV), F32),
        scratch_shapes=[
            pltpu.VMEM((rows, NV), F32),
            pltpu.VMEM((rows, NV), F32),
            pltpu.VMEM((rows, rank), BF16),
            pltpu.VMEM((NV, rows), BF16),
            pltpu.SemaphoreType.DMA((3,)),
        ],
        compiler_params=pltpu.CompilerParams(vmem_limit_bytes=12 * MIB),
        name="project",
    )(*in_hbm(x, y, basis))


def list_product(kernel, columns, list_ref, b):
    left = jnp.concatenate([kernel[b, n] for n in range(NBLK)], axis=1)
    right = jnp.concatenate([columns[list_ref[b, n]] for n in range(NBLK)], axis=0)
    return jnp.dot(left, right, preferred_element_type=F32)


def load_patch(slot, chunks, flat, sems):
    rows = chunks[0].shape[0]
    copies = []
    for k, chunk in enumerate(chunks):
        start = pl.multiple_of((slot ^ (k // 2)) * 2 * rows + (k % 2) * rows, rows)
        copies.append(pltpu.make_async_copy(chunk, flat.at[pl.ds(start, rows)], sems.at[k]))
        copies[-1].start()
    return copies


def split_all(flat, first, out, select):
    def split(block, carry):
        split_block(flat, pl.multiple_of(block * 2 * BLK, 2 * BLK), first + block, out, select)
        return carry

    count = flat.shape[0] // (2 * BLK)
    lax.fori_loop(0, count, split, 0, unroll=min(count, 16))


def own_body(slot_ref, *refs):
    chunks = refs[:4]
    out_ref, flat, sems = refs[4:]
    copies = load_patch(slot_ref[0] & 1, chunks, flat, sems)
    select = split_matrix()
    for copy in copies:
        copy.wait()
    split_all(flat, 0, out_ref, select)


def own_columns(slot, chunks):
    rows = chunks[0].shape[0]
    return pl.pallas_call(
        own_body,
        in_specs=[SMEM_SPEC] + [ANY_SPEC] * 4,
        out_specs=VMEM_SPEC,
        out_shape=pltpu.HBM((2 * rows // BLK, BLK, 2 * NV), BF16),
        scratch_shapes=[pltpu.VMEM((4 * rows, NV), BF16), pltpu.SemaphoreType.DMA((4,))],
        compiler_params=pltpu.CompilerParams(vmem_limit_bytes=8 * MIB),
        name="own_columns",
    )(slot, *chunks)


def far_body(slot_ref, *refs):
    chunks = refs[:2]
    out_ref, flat, sems = refs[2:]
    copies = load_patch(slot_ref[0] & 0, chunks, flat, sems)
    select = split_matrix()
    for copy in copies:
        copy.wait()
    split_all(flat, 0, out_ref, select)


def far_columns(slot, chunks):
    half = chunks[0].shape[0]
    return pl.pallas_call(
        far_body,
        in_specs=[SMEM_SPEC, ANY_SPEC, ANY_SPEC],
        out_specs=VMEM_SPEC,
        out_shape=pltpu.HBM((half // BLK, BLK, 2 * NV), BF16),
        scratch_shapes=[pltpu.VMEM((2 * half, NV), BF16), pltpu.SemaphoreType.DMA((2,))],
        compiler_params=pltpu.CompilerParams(vmem_limit_bytes=8 * MIB),
        name="far_columns",
    )(slot, *chunks)


def mirror_body(slot_ref, partner_ref, list_ref, *refs):
    chunks = refs[:8]
    kernel_hbm, out_ref, source, gathered, columns, kernel, sems, kernel_sems = refs[8:]
    copies = load_patch(slot_ref[0], chunks, source.reshape(2 * source.shape[0], NV), sems)
    blocks = kernel.shape[0]
    loads = [pltpu.make_async_copy(kernel_hbm.at[b], kernel.at[b], kernel_sems.at[b]) for b in range(blocks)]
    select = split_matrix()
    for copy in copies:
        copy.wait()
    for load in loads:
        load.start()
    unroll = 128

    def gather(step, carry):
        base = step * unroll
        for u in range(unroll):
            gathered[base + u] = source[partner_ref[0, base + u]]
        return carry

    lax.fori_loop(0, source.shape[0] // unroll, gather, 0)
    split_all(gathered.reshape(2 * gathered.shape[0], NV), 0, columns, select)
    for load in loads:
        load.wait()

    def product(b, carry):
        out_ref[b] = list_product(kernel, columns, list_ref, b)
        return carry

    lax.fori_loop(0, blocks, product, 0, unroll=4)


def mirror_product(slot, partner, indices, chunks, kernel):
    patch = partner.shape[1]
    blocks = kernel.shape[0]
    return pl.pallas_call(
        mirror_body,
        in_specs=[SMEM_SPEC] * 3 + [ANY_SPEC] * 9,
        out_specs=VMEM_SPEC,
        out_shape=jax.ShapeDtypeStruct((blocks, BLK, 2 * NV), F32),
        scratch_shapes=[
            pltpu.VMEM((patch, 2, NV), BF16),
            pltpu.VMEM((patch, 2, NV), BF16),
            pltpu.VMEM((patch // BLK, BLK, 2 * NV), BF16),
            pltpu.VMEM(kernel.shape, BF16),
            pltpu.SemaphoreType.DMA((8,)),
            pltpu.SemaphoreType.DMA((blocks,)),
        ],
        compiler_params=pltpu.CompilerParams(vmem_limit_bytes=24 * MIB),
        name="mirror_product",
    )(slot, partner, indices, *in_hbm(*chunks, kernel))


def column_of(row):
    return jnp.broadcast_to(row, (NV, NV)).T


def finish_body(last, slot_ref, list_ref, *refs):
    chunks = refs[:2]
    own_hbm, far_hbm, x_hbm, y_hbm, energy_ref, shift_ref, kernel_hbm, basis_hbm, weight_ref, mirror_ref = refs[2:12]
    rest = refs[12:]
    if last:
        next_x_hbm, next_y_hbm = rest[:2]
        rest = rest[2:]
    else:
        next_x_hbm, next_y_hbm, low_ref, high_ref, project_ref = rest[:5]
        rest = rest[5:]
    flat, columns, kernel, basis, x, y, levels, scratch, summed, chunk_sems, sems, save_sems = rest
    blocks = kernel.shape[0]
    copies = load_patch(slot_ref[0] & 0, chunks, flat, chunk_sems)
    count = own_hbm.shape[0]
    own_first = (slot_ref[0] // 2) * count
    far_count = far_hbm.shape[0]
    far_first = (slot_ref[0] ^ 2) * far_count
    extra = [
        pltpu.make_async_copy(own_hbm, columns.at[pl.ds(own_first, count)], chunk_sems.at[4]),
        pltpu.make_async_copy(far_hbm, columns.at[pl.ds(far_first, far_count)], chunk_sems.at[5]),
    ]
    for copy in extra:
        copy.start()

    def load(b, t):
        if t == 0:
            return pltpu.make_async_copy(kernel_hbm.at[b], kernel.at[b], sems.at[0, b])
        source, target = ((basis_hbm, basis), (x_hbm, x), (y_hbm, y))[t - 1]
        part = block_rows(b)
        return pltpu.make_async_copy(source.at[part], target.at[part], sems.at[t, b])

    def save(b, t):
        source, target = ((x, next_x_hbm), (y, next_y_hbm))[t]
        part = block_rows(b)
        return pltpu.make_async_copy(source.at[part], target.at[part], save_sems.at[t, b])

    half = BLK // 2
    for b in range(blocks):
        row = energy_ref[b]
        levels[b * BLK : b * BLK + half, :] = column_of(row[:, 0:half])
        levels[b * BLK + half : (b + 1) * BLK, :] = column_of(row[:, half:])
    for copy in copies:
        copy.wait()
    for b in range(blocks):
        for t in range(4):
            load(b, t).start()
    split_all(flat, (slot_ref[0] ^ 3) * far_count, columns, split_matrix())
    for copy in extra:
        copy.wait()
    shifts = shift_ref[...]
    for b in range(blocks):
        for t in range(4):
            load(b, t).wait()
        part = pl.ds(b * BLK, BLK)
        mirrored = mirror_ref[b]
        exchange = jnp.dot(basis[part, :], weight_ref[...], preferred_element_type=F32)
        direct = list_product(kernel, columns, list_ref, b)
        level = levels[part, :]
        next_x = x[part, :] + (direct[:, :NV] + mirrored[:, NV:] + exchange) / (level - shifts)
        next_y = y[part, :] + (direct[:, NV:] + mirrored[:, :NV] + exchange) / (level + shifts)
        x[part, :] = next_x
        y[part, :] = next_y
        for t in range(2):
            save(b, t).start()
        if not last:
            out_ref, place = (low_ref, b) if b < blocks // 2 else (high_ref, b - blocks // 2)
            out_ref[pl.ds(place * 2 * BLK, 2 * BLK), :] = interleave(next_x, next_y, scratch.at[b % 2])
            summed[:, b * BLK : (b + 1) * BLK] = add_vectors(next_x, next_y)
    if not last:
        store_projection(summed, basis, project_ref)
    for b in range(blocks):
        for t in range(2):
            save(b, t).wait()


def finish(last, slot, indices, chunks, own, far, x, y, energy, shift, kernel, basis, weights, mirrored):
    rows, rank = basis.shape
    blocks = kernel.shape[0]
    patch = 4 * rows
    out_specs = [ANY_SPEC, ANY_SPEC]
    out_shape = [pltpu.HBM((rows, NV), F32)] * 2
    if not last:
        out_specs += [VMEM_SPEC] * 3
        out_shape += [jax.ShapeDtypeStruct((rows, NV), BF16)] * 2 + [pltpu.HBM((rank, NV), F32)]

    def body(*refs):
        finish_body(last, *refs)

    return pl.pallas_call(
        body,
        in_specs=[SMEM_SPEC] * 2 + [ANY_SPEC] * 6 + [VMEM_SPEC] * 2 + [ANY_SPEC] * 2 + [VMEM_SPEC] * 2,
        out_specs=out_specs,
        out_shape=out_shape,
        scratch_shapes=[
            pltpu.VMEM((patch // 2, NV), BF16),
            pltpu.VMEM((patch // BLK, BLK, 2 * NV), BF16),
            pltpu.VMEM(kernel.shape, BF16),
            pltpu.VMEM(basis.shape, BF16),
            pltpu.VMEM((rows, NV), F32),
            pltpu.VMEM((rows, NV), F32),
            pltpu.VMEM((rows, NV), F32),
            pltpu.VMEM((2, 2 * BLK, NV), F32),
            pltpu.VMEM((NV, rows), BF16),
            pltpu.SemaphoreType.DMA((8,)),
            pltpu.SemaphoreType.DMA((4, blocks)),
            pltpu.SemaphoreType.DMA((2, blocks)),
        ],
        compiler_params=pltpu.CompilerParams(vmem_limit_bytes=32 * MIB),
        name="finish_last" if last else "finish",
    )(slot, indices, *in_hbm(*chunks, own, far, x, y), energy, shift, *in_hbm(kernel, basis), weights, mirrored)


def total_weights(partial):
    size = lax.axis_size(AXES)
    rank, vectors = partial.shape
    part = rank // size
    pieces = lax.all_to_all(partial.reshape(size, part, vectors), AXES, 0, 0, tiled=True)
    own = jnp.sum(pieces.astype(F32), axis=0).astype(BF16)
    spread = lax.all_to_all(jnp.broadcast_to(own[None], (size, part, vectors)), AXES, 0, 0, tiled=True)
    return spread.reshape(rank, vectors)


def on_device(x, y, energy, shift, res_kernel, res_list, cp_kernel, cp_list, partner, basis):
    size = lax.axis_size(AXES)
    narrow = lax.axis_size("narrow")
    near = size // 2
    far = near | (narrow // 2)
    slot = lax.axis_index("narrow").astype(jnp.int32).reshape(1)
    blocks = res_kernel.shape[0]
    levels = energy.reshape(blocks, 1, BLK)
    shifts = shift.reshape(1, NV)
    for app in range(APPS):
        last = app == APPS - 1
        if app == 0:
            low, high = pack(x, y)
            partial = project(x, y, basis)
        far_low = toggled(low, far)
        near_high = toggled(high, near)
        weights = total_weights(partial)
        far_high = toggled(high, far)
        near_low = toggled(low, near)
        own = [toggled(low, 1), toggled(high, 1)]
        across = [toggled(far_low, near), toggled(near_high, far)]
        near_swap = [toggled(near_low, 1), toggled(near_high, 1)]
        far_swap = [toggled(far_low, 1), toggled(far_high, 1)]
        mirror_chunks = [near_low, near_high] + near_swap + [far_low, far_high] + far_swap
        own_half = own_columns(slot, [low, high] + own)
        swapped = [toggled(c, 1) for c in across]
        far_half = far_columns(slot, across)
        mirrored = mirror_product(slot, partner, cp_list, mirror_chunks, cp_kernel)
        out = finish(
            last,
            slot,
            res_list,
            swapped,
            own_half,
            far_half,
            x,
            y,
            levels,
            shifts,
            res_kernel,
            basis,
            weights,
            mirrored,
        )
        if last:
            return tuple(out)
        x, y, low, high, partial = out


def solution(mesh):
    return jax.shard_map(
        on_device,
        mesh=mesh,
        in_specs=(
            P(AXES, None),
            P(AXES, None),
            P(AXES),
            P(),
            P(AXES, None, None, None),
            P(AXES, None),
            P(AXES, None, None, None),
            P(AXES, None),
            P("wide", None),
            P(AXES, None),
        ),
        out_specs=(P(AXES, None), P(AXES, None)),
        check_vma=False,
    )
```
